32 devices in a mesh: tg: 4 (over y, x), fft: 8 (over z, core).
Axes of the slice: x: 2, y: 2, z: 4, core: 2. Of those that a mesh axis runs over, the one named last changes fastest.
Arguments:
- coeffs: float32 [4, 2, 240, 2048], P(None, None, None, ('tg', 'fft')), may hold values from -6 to 6
- stick_count: int32 [32], replicated, may hold values from 16 to 64, as said below
- stick_column: int32 [2048], replicated, may hold values from 0 to 57599, as said below
- plane_owner: int32 [240], replicated, may hold values from 0 to 7, as said below
- potential: float32 [240, 57600], P('fft'), may hold values from -3 to 1
Outputs:
- applied: float32 [4, 2, 240, 2048], P(None, None, None, ('tg', 'fft'))
The draws below stay inside these ranges and needn't reach their ends.
Inputs may be any that keep to these rules, and one draw needn't show every extreme that they name: `stick_count`: each block of 64 slots holds at least 16 live sticks; max(1, 4 * 8 // 8) blocks are full in every draw. `stick_column`: all entries are distinct. `plane_owner`: no fft index owns more than 30 planes, and some own exactly 30.
All inputs are finite; a program needn't handle non-finite values.
Results may differ from the reference program's by a relative error of at most 0.000071.
Values sent between devices are 32-bit elements; how exact they have to be, the bound alone decides.
A program may use at most 256 MiB of HBM per device.

```python
import jax
import jax.numpy as jnp
from jax import lax

NX = 240
NY = 240
NZ = 240
BANDS = 4
S_MAX = 64
P_MAX = 30
SLOTS = 2048
PLANE_ROWS = 240
N_TG = 4
N_FFT = 8


def draw_stick_count(key, part):
    devices = N_TG * N_FFT
    low_key, pick_key = jax.random.split(jax.random.fold_in(key, 3))
    counts = jax.random.randint(low_key, (devices,), S_MAX // 4, S_MAX // 2 + 1)
    heavy_rows = jax.random.permutation(pick_key, devices)[:max(devices // 8, 1)]
    return counts.at[heavy_rows].set(S_MAX).astype(jnp.int32)


def draw_stick_column(key, part):
    shuffled = jax.random.permutation(jax.random.fold_in(key, 7), NX * NY)
    return shuffled[:N_TG * N_FFT * S_MAX].astype(jnp.int32)


def draw_plane_owner(key, part):
    plane_slots = (NZ + N_FFT - 1) // N_FFT
    total_slots = N_FFT * plane_slots
    dropped = total_slots - NZ
    drop_key, order_key = jax.random.split(jax.random.fold_in(key, 11))
    chosen = jax.random.permutation(drop_key, N_FFT)[:dropped]
    removed = jnp.zeros((total_slots,), jnp.int32).at[chosen * plane_slots + plane_slots - 1].set(1)
    retained = jnp.argsort(removed * total_slots + jnp.arange(total_slots, dtype=jnp.int32), stable=True)[:NZ]
    owners = (retained // plane_slots).astype(jnp.int32)
    placing = jax.random.permutation(order_key, NZ)
    return jnp.zeros((NZ,), jnp.int32).at[placing].set(owners)


def block_scale(rng, extent, shards, smallest, high):
    def one(dim, blocks):
        steps = jax.random.uniform(jax.random.fold_in(jax.random.fold_in(rng, 6), dim), (blocks,), jnp.float32, smallest / len(shards), high / len(shards))
        return jnp.repeat(jnp.exp(steps), extent[dim] // blocks).reshape((-1,) + (1,) * (len(extent) - dim - 1))

    factor_of = one(*shards[0])
    for cut in shards[1:]:
        factor_of = factor_of * one(*cut)
    return factor_of


def centred(rng, extent, width, most, cuts=(), kind=jnp.bfloat16):
    values = width * jax.random.normal(rng, extent, jnp.float32)
    if cuts:
        values = values * block_scale(rng, extent, cuts, -0.22, 0.18)
    return jnp.clip(values, -most, most).astype(kind)


def setup_inputs(seed: int = 0) -> dict:
    splits = jax.random.split(jax.random.key(seed), 6)
    coeffs = centred(splits[0], (BANDS, 2, NZ, SLOTS), 1.0, 6.0, ((3, 32),), jnp.float32)
    stick_count = draw_stick_count(jax.random.fold_in(splits[5], 71), 0)
    stick_column = draw_stick_column(jax.random.fold_in(splits[5], 71), 0)
    plane_owner = draw_plane_owner(jax.random.fold_in(splits[5], 71), 0)
    potential = jnp.clip(-3.0 + 4.0 * jax.random.uniform(splits[4], (PLANE_ROWS, NX * NY), jnp.float32) ** block_scale(splits[4], (PLANE_ROWS, NX * NY), ((0, 8),), -0.2, 0.2), -3.0, 1.0)
    return {"coeffs": coeffs, "stick_count": stick_count, "stick_column": stick_column, "plane_owner": plane_owner, "potential": potential}


def plane_rows_of(plane_owner, plane_slots):
    planes = jnp.arange(NZ, dtype=jnp.int32)
    same_owner = plane_owner[None, :] == plane_owner[:, None]
    earlier = planes[None, :] < planes[:, None]
    plane_ranks = jnp.sum((same_owner & earlier).astype(jnp.int32), axis=1)
    return plane_owner * plane_slots + plane_ranks


def reference(coeffs, stick_count, stick_column, plane_owner, potential):
    columns = NX * NY
    live_slots = (jnp.arange(S_MAX, dtype=jnp.int32)[None, :] < stick_count[:, None]).reshape(-1)
    target = jnp.where(live_slots, stick_column, columns)
    fetch_index = jnp.minimum(target, columns - 1)
    potential_grid = potential[plane_rows_of(plane_owner, P_MAX)].reshape(NZ, NX, NY)

    def one_band(coefficient):
        real_grid = jnp.zeros((NZ, columns), coefficient.dtype).at[:, target].add(coefficient[0], mode="drop")
        imag_grid = jnp.zeros((NZ, columns), coefficient.dtype).at[:, target].add(coefficient[1], mode="drop")
        spectrum = lax.complex(real_grid, imag_grid).reshape(NZ, NX, NY)
        wave_grid = jnp.fft.ifftn(spectrum, norm="ortho")
        applied = jnp.fft.fftn(wave_grid * potential_grid, norm="ortho").reshape(NZ, columns)
        picked = applied[:, fetch_index]
        return jnp.stack([jnp.where(live_slots, jnp.real(picked), 0.0), jnp.where(live_slots, jnp.imag(picked), 0.0)])

    return lax.map(one_band, coeffs)
```

```python
import functools
import math

import jax
import jax.numpy as jnp
import ml_dtypes
import numpy as np
from jax import lax
from jax.experimental import pallas as pl
from jax.experimental.pallas import tpu as pltpu
from jax.sharding import PartitionSpec as P

NX = 240
NY = 240
NZ = 240
PAD = 256
FOLD = 128
LANES = 64
RADIX = 16
ODD = 15
COMBOS = RADIX * RADIX
SLOTS = 8
GROUP = 8
MESH = pl.DeviceIdType.MESH


def split_table(table):
    table = table.astype(np.float32)
    high = table.astype(ml_dtypes.bfloat16)
    low = (table - high.astype(np.float32)).astype(ml_dtypes.bfloat16)
    return np.stack([high, low])


def z_table():
    indices = np.arange(NZ)
    angles = (indices[:, None] * indices[None, :] % NZ) * (2.0 * math.pi / NZ)
    table = np.zeros((PAD, 2 * PAD))
    table[:NZ, :NZ] = np.cos(angles) / math.sqrt(NZ)
    table[:NZ, PAD : PAD + NZ] = np.sin(angles) / math.sqrt(NZ)
    return split_table(table)


def folded_table():
    first = np.arange(ODD)
    table = np.zeros((PAD, PAD))
    for bx in range(ODD // 2 + 1):
        for by in range(ODD if bx else ODD // 2 + 1):
            i = ODD // 2 + 1 + (bx - 1) * ODD + by if bx else by
            angles = ((bx * first[:, None] + by * first[None, :]) % ODD) * (2.0 * math.pi / ODD)
            wide = np.zeros((2, RADIX, RADIX))
            wide[0, :ODD, :ODD] = np.cos(angles)
            wide[1, :ODD, :ODD] = -np.sin(angles)
            table[i] = wide[0].reshape(-1) / NX
            table[FOLD + i] = wide[1].reshape(-1) / NX
    return split_table(table)


def y_order():
    order = np.zeros((PAD, PAD), np.float32)
    y = np.arange(NY)
    order[y, (-y) % RADIX * RADIX + y % ODD] = 1.0
    return order.astype(ml_dtypes.bfloat16)


def halves(values):
    high = values.astype(jnp.bfloat16)
    low = (values - high.astype(jnp.float32)).astype(jnp.bfloat16)
    return high, low


def dot(a, b):
    return jnp.dot(a, b, preferred_element_type=jnp.float32)


def dot_last(a, b):
    return lax.dot_general(a, b, (((1,), (1,)), ((), ())), preferred_element_type=jnp.float32)


def butterfly(real, imag, sign):
    def four(xs):
        (ar, ai), (br, bi), (cr, ci), (dr, di) = xs
        er, ei, fr, fi = ar + cr, ai + ci, ar - cr, ai - ci
        gr, gi, hr, hi = br + dr, bi + di, br - dr, bi - di
        if sign > 0:
            return [(er + gr, ei + gi), (fr - hi, fi + hr), (er - gr, ei - gi), (fr + hi, fi - hr)]
        return [(er + gr, ei + gi), (fr + hi, fi - hr), (er - gr, ei - gi), (fr - hi, fi + hr)]

    def turn(x, power):
        r, i = x
        root = math.sqrt(0.5)
        if power == 0:
            return x
        if power == 4:
            return (-i, r) if sign > 0 else (i, -r)
        if power == 2:
            return ((r - i) * root, (r + i) * root) if sign > 0 else ((r + i) * root, (i - r) * root)
        if power == 6:
            return ((r + i) * -root, (r - i) * root) if sign > 0 else ((i - r) * root, (r + i) * -root)
        c = math.cos(2 * math.pi * power / 16)
        s = math.sin(2 * math.pi * power / 16) * sign
        return r * c - i * s, r * s + i * c

    inner = [four([(real[4 * n1 + n2], imag[4 * n1 + n2]) for n1 in range(4)]) for n2 in range(4)]
    out_real, out_imag = [None] * 16, [None] * 16
    for k1 in range(4):
        outer = four([turn(inner[n2][k1], n2 * k1) for n2 in range(4)])
        for k2 in range(4):
            out_real[k1 + 4 * k2], out_imag[k1 + 4 * k2] = outer[k2]
    return out_real, out_imag


def swap_halves(first, second):
    lower = lax.broadcasted_iota(jnp.int32, first.shape, first.ndim - 1) < 64
    first_turned = pltpu.roll(first, 64, first.ndim - 1)
    second_turned = pltpu.roll(second, 64, second.ndim - 1)
    return jnp.where(lower, first, second_turned), jnp.where(lower, first_turned, second)


def grid_kernel(
    source_ref, row_ref, half_ref, count_ref, sticks_ref, local_ref, table_ref, turned_ref, out_ref,
    columns, waves, staged,
):
    devices = sticks_ref.shape[0]
    rows = devices * 32
    lane_half = lax.broadcasted_iota(jnp.int32, (1, 128), 1) // 64

    def clear(i, carry):
        columns[pl.ds(pl.multiple_of(i * PAD, PAD), PAD), :] = jnp.zeros((PAD, 128), jnp.float32)
        return carry

    lax.fori_loop(0, COMBOS // 2, clear, 0)

    def arrange(quad, carry):
        lines = [None] * 16
        for pair in range(2):
            d = quad * 4 + pair * 2
            for c in range(2):
                for t in range(2):
                    at = (pl.ds(c * 8, 8), pl.ds(t * 128, 128))
                    even, odd = swap_halves(sticks_ref[d, at[0], at[1]], sticks_ref[d + 1, at[0], at[1]])
                    lines[pair * 8 + c * 4 + t * 2] = even
                    lines[pair * 8 + c * 4 + t * 2 + 1] = odd
        block = jnp.concatenate(lines, axis=0).T
        base = pl.multiple_of(quad * 128, 128)
        staged[pl.ds(base, 128), :] = block
        staged[pl.ds(rows + base, 128), :] = pltpu.roll(block, 64, 1)
        return carry

    lax.fori_loop(0, devices // 4, arrange, 0)

    def over_live(work):
        def per_device(d, carry):
            def per_group(i, inner):
                for j in range(GROUP):
                    work(d * 64 + i * GROUP + j)
                return inner

            return lax.fori_loop(0, (count_ref[d] + GROUP - 1) // GROUP, per_group, carry)

        lax.fori_loop(0, devices, per_device, 0)

    def scatter(g):
        value = staged[pl.ds(source_ref[g], 1), :]
        pltpu.store(columns.at[pl.ds(row_ref[g], 1), :], value, mask=lane_half == half_ref[g])

    over_live(scatter)

    def swapped(values):
        grid = values.reshape(2, 2, LANES // 2, FOLD)
        return grid[:, 0], grid[:, 1]

    def joined(real, imag):
        return jnp.stack([real, imag], axis=1).reshape(128, FOLD)

    def forward(block, carry):
        base = pl.multiple_of(block * PAD, PAD)
        low_half = columns[pl.ds(base, FOLD), :]
        high_half = columns[pl.ds(base + FOLD, FOLD), :]
        even = (low_half + high_half).T
        odd_real, odd_imag = swapped((low_half - high_half).T)
        values = jnp.concatenate([even, joined(odd_imag, -odd_real)], axis=1)
        high, low = halves(values)
        total = dot(high, table_ref[0]) + dot(high, table_ref[1]) + dot(low, table_ref[0])
        waves[pl.ds(pl.multiple_of(block * 128, 128), 128), :] = total
        return carry

    lax.fori_loop(0, COMBOS // 2, forward, 0, unroll=8)

    def place(combo, c, b):
        return pl.ds(pl.multiple_of(combo * LANES, LANES) + c * 32 + b * 8, 8)

    def along_x(sign):
        def step(ay, carry):
            for b in range(4):
                for lanes in (pl.ds(0, 128), pl.ds(128, 128)):
                    real = [waves[place(k * RADIX + ay, 0, b), lanes] for k in range(RADIX)]
                    imag = [waves[place(k * RADIX + ay, 1, b), lanes] for k in range(RADIX)]
                    real, imag = butterfly(real, imag, sign)
                    for k in range(RADIX):
                        waves[place(k * RADIX + ay, 0, b), lanes] = real[k]
                        waves[place(k * RADIX + ay, 1, b), lanes] = imag[k]
            return carry

        lax.fori_loop(0, RADIX, step, 0)

    along_x(1)

    def along_y(ax, carry):
        for lanes in (pl.ds(0, 128), pl.ds(128, 128)):
            for b in range(4):
                real = [waves[place(ax * RADIX + k, 0, b), lanes] for k in range(RADIX)]
                imag = [waves[place(ax * RADIX + k, 1, b), lanes] for k in range(RADIX)]
                real, imag = butterfly(real, imag, 1)
                local = [local_ref[ax * RADIX + k, :, lanes] for k in range(RADIX)]
                real = [value * local[k] for k, value in enumerate(real)]
                imag = [value * local[k] for k, value in enumerate(imag)]
                real, imag = butterfly(real, imag, -1)
                for k in range(RADIX):
                    waves[place(ax * RADIX + k, 0, b), lanes] = real[k]
                    waves[place(ax * RADIX + k, 1, b), lanes] = imag[k]
        return carry

    lax.fori_loop(0, RADIX, along_y, 0)
    along_x(-1)

    def backward(block, carry):
        high, low = halves(waves[pl.ds(pl.multiple_of(block * 128, 128), 128), :])
        total = dot(high, turned_ref[0]) + dot(high, turned_ref[1]) + dot(low, turned_ref[0])
        cosine = total[:, :FOLD]
        sine_real, sine_imag = swapped(total[:, FOLD:])
        sine = joined(sine_imag, -sine_real)
        base = pl.multiple_of(block * PAD, PAD)
        columns[pl.ds(base, FOLD), :] = (cosine - sine).T
        columns[pl.ds(base + FOLD, FOLD), :] = (cosine + sine).T
        return carry

    lax.fori_loop(0, COMBOS // 2, backward, 0, unroll=8)
    staged[...] = jnp.zeros_like(staged)

    def gather(g):
        value = columns[pl.ds(row_ref[g], 1), :]
        pltpu.store(staged.at[pl.ds(source_ref[g], 1), :], value, mask=lane_half == half_ref[g])

    over_live(gather)

    def restore(quad, carry):
        base = pl.multiple_of(quad * 128, 128)
        block = staged[pl.ds(base, 128), :] + pltpu.roll(staged[pl.ds(rows + base, 128), :], 64, 1)
        block = block.T
        for pair in range(2):
            d = quad * 4 + pair * 2
            for c in range(2):
                for t in range(2):
                    line = (pair * 8 + c * 4 + t * 2) * 8
                    first, second = swap_halves(block[line : line + 8], block[line + 8 : line + 16])
                    at = (pl.ds(c * 8, 8), pl.ds(t * 128, 128))
                    out_ref[d, at[0], at[1]] = first
                    out_ref[d + 1, at[0], at[1]] = second
        return carry

    lax.fori_loop(0, devices // 4, restore, 0)


def on_grid(source, row, half, count, sticks, local):
    table = folded_table()
    turned = np.swapaxes(table, 1, 2)
    rows = sticks.shape[0] * 32
    smem = pl.BlockSpec(memory_space=pltpu.SMEM)
    vmem = pl.BlockSpec(memory_space=pltpu.VMEM)
    return pl.pallas_call(
        grid_kernel,
        out_shape=jax.ShapeDtypeStruct(sticks.shape, jnp.float32),
        in_specs=[smem] * 4 + [vmem] * 4,
        out_specs=vmem,
        scratch_shapes=[
            pltpu.VMEM((COMBOS // 2 * PAD, 128), jnp.float32),
            pltpu.VMEM((COMBOS * LANES, PAD), jnp.float32),
            pltpu.VMEM((2 * rows, 128), jnp.float32),
        ],
        compiler_params=pltpu.CompilerParams(vmem_limit_bytes=60 * 2**20),
    )(source, row, half, count, sticks, local, jnp.asarray(table), jnp.asarray(turned))


class Layout:
    def __init__(self, tg_size, fft_size, plane_slots):
        self.tg_size, self.fft_size, self.plane_slots = tg_size, fft_size, plane_slots
        self.devices = tg_size * fft_size
        self.chunk = -(-plane_slots // tg_size)
        self.starts = [t * self.chunk // SLOTS * SLOTS for t in range(tg_size)]


def greet(n, fft_size, me):
    barrier = pltpu.get_barrier_semaphore()

    def signal(i, carry):
        other = lax.rem(me + i, n)
        pl.semaphore_signal(
            barrier, inc=1, device_id=(other // fft_size, lax.rem(other, fft_size)), device_id_type=MESH
        )
        return carry

    lax.fori_loop(1, n, signal, 0)
    return lambda: pl.semaphore_wait(barrier, n - 1)


def exchange(n, fft_size, me, source, target, send_sem, recv_sem):
    def copy(i):
        other = lax.rem(me + i, n)
        return pltpu.make_async_remote_copy(
            src_ref=source.at[other], dst_ref=target.at[me], send_sem=send_sem.at[i], recv_sem=recv_sem.at[i],
            device_id=(other // fft_size, lax.rem(other, fft_size)), device_id_type=MESH,
        )

    def start(i, carry):
        copy(i).start()
        return carry

    def wait(i, carry):
        copy(i).wait()
        return carry

    own = pltpu.make_async_copy(source.at[me], target.at[me], send_sem.at[0])

    def begin():
        lax.fori_loop(1, n, start, 0)
        own.start()

    def finish():
        own.wait()
        lax.fori_loop(1, n, wait, 0)

    return begin, finish


def plane_tables(layout, owner_ref, table_ref, first):
    owner = jnp.broadcast_to(owner_ref[...], (PAD, PAD)).astype(jnp.float32)
    index = lax.broadcasted_iota(jnp.int32, (PAD, PAD), 0)
    same = (owner == owner.T) & (index < lax.broadcasted_iota(jnp.int32, (PAD, PAD), 1))
    rank = jnp.sum(jnp.where(same, 1.0, 0.0), axis=0, keepdims=True)
    group = jnp.zeros_like(rank)
    offset = jnp.zeros_like(rank)
    for t in range(1, layout.tg_size):
        beyond = rank >= float(t * layout.chunk)
        group = jnp.where(beyond, float(t), group)
        offset = jnp.where(beyond, float(layout.starts[t]), offset)
    row = (group * layout.fft_size + owner[:1]) * SLOTS + rank - offset
    pick = jnp.where(index.astype(jnp.float32) + float(first) == row, 1.0, 0.0).astype(jnp.bfloat16)
    return dot(pick, table_ref[0]).astype(jnp.bfloat16), dot(pick, table_ref[1]).astype(jnp.bfloat16)


def lift_kernel(
    layout, coeffs_ref, owner_ref, potential_ref, table_ref, order_ref, out_ref, local_ref,
    parts, slab, lines, spread, send_sem, recv_sem, slab_sem,
):
    n, fft_size = layout.devices, layout.fft_size
    tg = lax.axis_index("tg")
    me = tg * fft_size + lax.axis_index("fft")
    greeted = greet(n, fft_size, me)

    slabs = []
    for t in range(layout.tg_size):
        start = layout.starts[t]
        count = min(SLOTS, layout.plane_slots - start)
        slabs.append((t, count, pltpu.make_async_copy(
            potential_ref.at[pl.ds(start, count), :], slab.at[pl.ds(0, count), :], slab_sem
        )))
    for t, count, copy in slabs:
        @pl.when(tg == t)
        def _():
            if count < SLOTS:
                slab[...] = jnp.zeros_like(slab)
            copy.start()

    bands, _, sticks, _ = coeffs_ref.shape
    real = halves(coeffs_ref[:, 0].reshape(bands * sticks, NZ))
    imag = halves(coeffs_ref[:, 1].reshape(bands * sticks, NZ))

    def three(high, low, values):
        return dot_last(high, values[0]) + dot_last(low, values[0]) + dot_last(high, values[1])

    per = PAD // SLOTS
    for first in range(0, n, per):
        high, low = plane_tables(layout, owner_ref, table_ref, first * SLOTS)
        cos_high, cos_low = high[:, :NZ], low[:, :NZ]
        sin_high, sin_low = high[:, PAD : PAD + NZ], low[:, PAD : PAD + NZ]
        up_real = three(cos_high, cos_low, real) - three(sin_high, sin_low, imag)
        up_imag = three(sin_high, sin_low, real) + three(cos_high, cos_low, imag)
        parts[first : first + per, :SLOTS] = up_real.reshape(per, SLOTS, bands * sticks)
        parts[first : first + per, SLOTS:] = up_imag.reshape(per, SLOTS, bands * sticks)

    begin, finish = exchange(n, fft_size, me, parts, out_ref, send_sem, recv_sem)
    greeted()
    begin()

    for t, count, copy in slabs:
        @pl.when(tg == t)
        def _():
            copy.wait()

    lines[:, NY:] = jnp.zeros((NX * SLOTS, PAD - NY), jnp.float32)

    def cut(q, carry):
        wide = slab[:, pl.ds(pl.multiple_of(q * 8 * NY, 128), 8 * NY)]
        for r in range(8):
            lines[pl.ds(pl.multiple_of(q * 8 * SLOTS, 8 * SLOTS) + r * SLOTS, SLOTS), :NY] = wide[:, r * NY : (r + 1) * NY]
        return carry

    lax.fori_loop(0, NX // 8, cut, 0)
    order = order_ref[...]

    def reorder(i, carry):
        at = pl.ds(pl.multiple_of(i * 128, 128), 128)
        values = lines[at, :]
        high, low = halves(values)
        rest = (values - high.astype(jnp.float32) - low.astype(jnp.float32)).astype(jnp.bfloat16)
        spread[at, :] = dot(high, order) + dot(low, order) + dot(rest, order)
        return carry

    lax.fori_loop(0, NX * SLOTS // 128, reorder, 0)
    lane_block = lax.broadcasted_iota(jnp.int32, (SLOTS, 128), 1) // RADIX

    def regroup(nx, carry):
        tiles = []
        for mx in range(ODD):
            x = lax.rem(nx * ODD + mx * RADIX, NX)
            at = pl.ds(pl.multiple_of(x * SLOTS, SLOTS), SLOTS)
            tiles.append([spread[at, :128], spread[at, 128:]])
        tiles.append([jnp.zeros((SLOTS, 128), jnp.float32)] * 2)
        tiles = [[tiles[m % 8 + 8 * (h % 2)][m // 8] for h in range(2)] for m in range(16)]
        for bit in (4, 2, 1):
            shift = bit * RADIX
            clear = lane_block % (2 * bit) < bit
            fresh = [[None, None] for _ in range(16)]
            for m in range(16):
                if m & bit:
                    continue
                for h in range(2):
                    a, b = tiles[m][h], tiles[m | bit][h]
                    fresh[m][h] = jnp.where(clear, a, pltpu.roll(b, shift, 1))
                    fresh[m | bit][h] = jnp.where(clear, pltpu.roll(a, 128 - shift, 1), b)
            tiles = fresh
        for ny in range(16):
            local_ref[nx * RADIX + ny, :, :128] = tiles[ny][0]
            local_ref[nx * RADIX + ny, :, 128:] = tiles[ny][1]
        return carry

    lax.fori_loop(0, RADIX, regroup, 0)
    finish()


def lift(layout, coeffs, owner, potential):
    bands, _, sticks, _ = coeffs.shape
    n = layout.devices
    hbm = pl.BlockSpec(memory_space=pl.ANY)
    vmem = pl.BlockSpec(memory_space=pltpu.VMEM)
    return pl.pallas_call(
        functools.partial(lift_kernel, layout),
        out_shape=(
            jax.ShapeDtypeStruct((n, 2 * SLOTS, bands * sticks), jnp.float32),
            jax.ShapeDtypeStruct((COMBOS, SLOTS, PAD), jnp.float32),
        ),
        in_specs=[vmem, vmem, hbm, vmem, vmem],
        out_specs=(hbm, vmem),
        scratch_shapes=[
            pltpu.VMEM((n, 2 * SLOTS, bands * sticks), jnp.float32),
            pltpu.VMEM((SLOTS, NX * NY), jnp.float32),
            pltpu.VMEM((NX * SLOTS, PAD), jnp.float32),
            pltpu.VMEM((NX * SLOTS, PAD), jnp.float32),
            pltpu.SemaphoreType.DMA((n,)),
            pltpu.SemaphoreType.DMA((n,)),
            pltpu.SemaphoreType.DMA,
        ],
        compiler_params=pltpu.CompilerParams(
            collective_id=0, has_side_effects=True, vmem_limit_bytes=48 * 2**20
        ),
    )(coeffs, owner, potential, jnp.asarray(z_table()), jnp.asarray(y_order()))


def back_kernel(layout, worked_ref, owner_ref, count_ref, table_ref, out_ref, received, send_sem, recv_sem):
    n, fft_size = layout.devices, layout.fft_size
    me = lax.axis_index("tg") * fft_size + lax.axis_index("fft")
    begin, finish = exchange(n, fft_size, me, worked_ref, received, send_sem, recv_sem)
    greet(n, fft_size, me)()
    begin()
    per = PAD // SLOTS
    tables = [plane_tables(layout, owner_ref, table_ref, first * SLOTS) for first in range(0, n, per)]
    finish()

    bands, _, sticks, _ = out_ref.shape
    out_real = jnp.zeros((bands * sticks, PAD), jnp.float32)
    out_imag = jnp.zeros((bands * sticks, PAD), jnp.float32)

    def three(values, high, low):
        return dot(values[0], high) + dot(values[0], low) + dot(values[1], high)

    for index, first in enumerate(range(0, n, per)):
        high, low = tables[index]
        real = halves(received[first : first + per, :SLOTS].reshape(PAD, bands * sticks).T)
        imag = halves(received[first : first + per, SLOTS:].reshape(PAD, bands * sticks).T)
        cos_high, cos_low = high[:, :PAD], low[:, :PAD]
        sin_high, sin_low = high[:, PAD:], low[:, PAD:]
        out_real += three(real, cos_high, cos_low) + three(imag, sin_high, sin_low)
        out_imag += three(imag, cos_high, cos_low) - three(real, sin_high, sin_low)
    live = lax.broadcasted_iota(jnp.int32, (bands, sticks, NZ), 1) < count_ref[me]
    out_ref[:, 0] = jnp.where(live, out_real[:, :NZ].reshape(bands, sticks, NZ), 0.0)
    out_ref[:, 1] = jnp.where(live, out_imag[:, :NZ].reshape(bands, sticks, NZ), 0.0)


def lower(layout, worked, owner, count, shape):
    n = layout.devices
    hbm = pl.BlockSpec(memory_space=pl.ANY)
    vmem = pl.BlockSpec(memory_space=pltpu.VMEM)
    return pl.pallas_call(
        functools.partial(back_kernel, layout),
        out_shape=jax.ShapeDtypeStruct(shape, jnp.float32),
        in_specs=[hbm, vmem, pl.BlockSpec(memory_space=pltpu.SMEM), vmem],
        out_specs=vmem,
        scratch_shapes=[
            pltpu.VMEM(worked.shape, jnp.float32),
            pltpu.SemaphoreType.DMA((n,)),
            pltpu.SemaphoreType.DMA((n,)),
        ],
        compiler_params=pltpu.CompilerParams(
            collective_id=1, has_side_effects=True, vmem_limit_bytes=48 * 2**20
        ),
    )(worked, owner, count, jnp.asarray(z_table()))


def stick_places(stick_count, stick_column, slot_count, devices):
    slot = jnp.arange(slot_count, dtype=jnp.int32)
    live = (slot[None, :] < stick_count[:, None]).reshape(-1)
    x, y = stick_column // NY, stick_column % NY
    combo = x % RADIX * RADIX + y % RADIX
    bx, by = x % ODD, y % ODD
    negative = (bx > ODD // 2) | ((bx == 0) & (by > ODD // 2))
    bx = jnp.where(negative & (bx > 0), ODD - bx, bx)
    by = jnp.where(negative & (by > 0), ODD - by, by)
    place = jnp.where(bx == 0, by, ODD // 2 + 1 + (bx - 1) * ODD + by) + jnp.where(negative, FOLD, 0)
    row = jnp.where(live, combo // 2 * PAD + place, FOLD - 1)
    half = combo % 2
    glob = jnp.arange(devices * slot_count, dtype=jnp.int32)
    device, within = glob // slot_count, glob % slot_count
    source = device // 4 * 128 + device % 2 * 64 + within
    source = source + jnp.where(device // 2 % 2 != half, devices * slot_count // 2, 0)
    return source, row, half


def per_device(coeffs, stick_count, stick_column, plane_owner, potential):
    layout = Layout(lax.axis_size("tg"), lax.axis_size("fft"), potential.shape[0])
    slot_count = coeffs.shape[3]
    turned = jnp.swapaxes(coeffs, 2, 3)
    owner = jnp.pad(plane_owner, (0, PAD - NZ), constant_values=layout.fft_size * 2).reshape(1, PAD)
    sticks, local = lift(layout, turned, owner, potential)
    source, row, half = stick_places(stick_count, stick_column, slot_count, layout.devices)
    worked = on_grid(source, row, half, stick_count, sticks, local)
    applied = lower(layout, worked, owner, stick_count, turned.shape)
    return jnp.swapaxes(applied, 2, 3)


def solution(mesh):
    in_specs = (P(None, None, None, ("tg", "fft")), P(), P(), P(), P("fft", None))
    out_specs = P(None, None, None, ("tg", "fft"))
    return jax.shard_map(
        per_device, mesh=mesh, in_specs=in_specs, out_specs=out_specs, check_vma=False
    )
```

```python
import functools
import math

import jax
import jax.numpy as jnp
import ml_dtypes
import numpy as np
from jax import lax
from jax.experimental import pallas as pl
from jax.experimental.pallas import tpu as pltpu
from jax.sharding import PartitionSpec as P

NX = 240
NY = 240
NZ = 240
PAD = 256
FOLD = 128
LANES = 64
RADIX = 16
ODD = 15
COMBOS = RADIX * RADIX
SLOTS = 8
GROUP = 8
UNROLL_Y = 2
MESH = pl.DeviceIdType.MESH


def split_table(table):
    table = table.astype(np.float32)
    high = table.astype(ml_dtypes.bfloat16)
    low = (table - high.astype(np.float32)).astype(ml_dtypes.bfloat16)
    return np.stack([high, low])


def z_table():
    indices = np.arange(NZ)
    angles = (indices[:, None] * indices[None, :] % NZ) * (2.0 * math.pi / NZ)
    table = np.zeros((PAD, 2 * PAD))
    table[:NZ, :NZ] = np.cos(angles) / math.sqrt(NZ)
    table[:NZ, PAD : PAD + NZ] = np.sin(angles) / math.sqrt(NZ)
    return split_table(table)


def folded_table():
    first = np.arange(ODD)
    table = np.zeros((PAD, PAD))
    for bx in range(ODD // 2 + 1):
        for by in range(ODD if bx else ODD // 2 + 1):
            i = ODD // 2 + 1 + (bx - 1) * ODD + by if bx else by
            angles = ((bx * first[:, None] + by * first[None, :]) % ODD) * (2.0 * math.pi / ODD)
            wide = np.zeros((2, RADIX, RADIX))
            wide[0, :ODD, :ODD] = np.cos(angles)
            wide[1, :ODD, :ODD] = -np.sin(angles)
            table[i] = wide[0].reshape(-1) / NX
            table[FOLD + i] = wide[1].reshape(-1) / NX
    return split_table(table)


def y_order():
    order = np.zeros((PAD, PAD), np.float32)
    y = np.arange(NY)
    order[y, (-y) % RADIX * RADIX + y % ODD] = 1.0
    return order.astype(ml_dtypes.bfloat16)


def halves(values):
    high = values.astype(jnp.bfloat16)
    low = (values - high.astype(jnp.float32)).astype(jnp.bfloat16)
    return high, low


def dot(a, b):
    return jnp.dot(a, b, preferred_element_type=jnp.float32)


def dot_last(a, b):
    return lax.dot_general(a, b, (((1,), (1,)), ((), ())), preferred_element_type=jnp.float32)


def butterfly(real, imag, sign):
    def four(xs):
        (ar, ai), (br, bi), (cr, ci), (dr, di) = xs
        er, ei, fr, fi = ar + cr, ai + ci, ar - cr, ai - ci
        gr, gi, hr, hi = br + dr, bi + di, br - dr, bi - di
        if sign > 0:
            return [(er + gr, ei + gi), (fr - hi, fi + hr), (er - gr, ei - gi), (fr + hi, fi - hr)]
        return [(er + gr, ei + gi), (fr + hi, fi - hr), (er - gr, ei - gi), (fr - hi, fi + hr)]

    def turn(x, power):
        r, i = x
        root = math.sqrt(0.5)
        if power == 0:
            return x
        if power == 4:
            return (-i, r) if sign > 0 else (i, -r)
        if power == 2:
            return ((r - i) * root, (r + i) * root) if sign > 0 else ((r + i) * root, (i - r) * root)
        if power == 6:
            return ((r + i) * -root, (r - i) * root) if sign > 0 else ((i - r) * root, (r + i) * -root)
        c = math.cos(2 * math.pi * power / 16)
        s = math.sin(2 * math.pi * power / 16) * sign
        return r * c - i * s, r * s + i * c

    inner = [four([(real[4 * n1 + n2], imag[4 * n1 + n2]) for n1 in range(4)]) for n2 in range(4)]
    out_real, out_imag = [None] * 16, [None] * 16
    for k1 in range(4):
        outer = four([turn(inner[n2][k1], n2 * k1) for n2 in range(4)])
        for k2 in range(4):
            out_real[k1 + 4 * k2], out_imag[k1 + 4 * k2] = outer[k2]
    return out_real, out_imag


def swap_halves(first, second):
    lower = lax.broadcasted_iota(jnp.int32, first.shape, first.ndim - 1) < 64
    first_turned = pltpu.roll(first, 64, first.ndim - 1)
    second_turned = pltpu.roll(second, 64, second.ndim - 1)
    return jnp.where(lower, first, second_turned), jnp.where(lower, first_turned, second)


def grid_kernel(
    source_ref, row_ref, half_ref, count_ref, sticks_ref, local_ref, table_ref, turned_ref, out_ref,
    columns, waves, ring, staged,
):
    devices = sticks_ref.shape[0]
    rows = devices * 32
    lane_half = lax.broadcasted_iota(jnp.int32, (1, 128), 1) // 64

    def clear(i, carry):
        columns[pl.ds(pl.multiple_of(i * PAD, PAD), PAD), :] = jnp.zeros((PAD, 128), jnp.float32)
        return carry

    lax.fori_loop(0, COMBOS // 2, clear, 0)

    def arrange(quad, carry):
        lines = [None] * 16
        for pair in range(2):
            d = quad * 4 + pair * 2
            for c in range(2):
                for t in range(2):
                    at = (pl.ds(c * 8, 8), pl.ds(t * 128, 128))
                    even, odd = swap_halves(sticks_ref[d, at[0], at[1]], sticks_ref[d + 1, at[0], at[1]])
                    lines[pair * 8 + c * 4 + t * 2] = even
                    lines[pair * 8 + c * 4 + t * 2 + 1] = odd
        block = jnp.concatenate(lines, axis=0).T
        base = pl.multiple_of(quad * 128, 128)
        staged[pl.ds(base, 128), :] = block
        staged[pl.ds(rows + base, 128), :] = pltpu.roll(block, 64, 1)
        return carry

    lax.fori_loop(0, devices // 4, arrange, 0, unroll=4)

    def over_live(work):
        def per_device(d, carry):
            def per_group(i, inner):
                for j in range(GROUP):
                    work(d * 64 + i * GROUP + j)
                return inner

            return lax.fori_loop(0, (count_ref[d] + GROUP - 1) // GROUP, per_group, carry)

        lax.fori_loop(0, devices, per_device, 0)

    def scatter(g):
        value = staged[pl.ds(source_ref[g], 1), :]
        pltpu.store(columns.at[pl.ds(row_ref[g], 1), :], value, mask=lane_half == half_ref[g])

    over_live(scatter)

    def forward(i, ax):
        base = pl.multiple_of((ax * (RADIX // 2) + i) * PAD, PAD)
        low_half = columns[pl.ds(base, FOLD), :].T
        high_half = columns[pl.ds(base + FOLD, FOLD), :].T
        odd = []
        for h in range(2):
            re, im = slice(h * 64, h * 64 + 32), slice(h * 64 + 32, h * 64 + 64)
            odd += [low_half[im] - high_half[im], high_half[re] - low_half[re]]
        values = jnp.concatenate([low_half + high_half, jnp.concatenate(odd, axis=0)], axis=1)
        high, low = halves(values)
        total = dot(high, table_ref[0]) + dot(high, table_ref[1]) + dot(low, table_ref[0])
        for l in range(2):
            ring[pl.ds(pl.multiple_of((l * RADIX + ax) * 128, 128), 128), :] = total[:, l * 128 : (l + 1) * 128]

    def in_ring(unit, k, c):
        h, b, l = unit // 8, unit // 2 % 4, unit % 2
        return pl.ds((l * RADIX + k) * 128 + h * 64 + c * 32 + b * 8, 8)

    def in_grid(i, unit, k, c):
        h, b, l = unit // 8, unit // 2 % 4, unit % 2
        base = pl.multiple_of(2 * i * LANES, 128)
        return pl.ds(base + (l * COMBOS + k * RADIX + h) * LANES + c * 32 + b * 8, 8)

    def forward_x(i, unit):
        real = [ring[in_ring(unit, k, 0), :] for k in range(RADIX)]
        imag = [ring[in_ring(unit, k, 1), :] for k in range(RADIX)]
        real, imag = butterfly(real, imag, 1)
        for k in range(RADIX):
            waves[in_grid(i, unit, k, 0), :] = real[k]
            waves[in_grid(i, unit, k, 1), :] = imag[k]

    def backward_x(i, unit):
        real = [columns[in_grid(i, unit, k, 0), :] for k in range(RADIX)]
        imag = [columns[in_grid(i, unit, k, 1), :] for k in range(RADIX)]
        real, imag = butterfly(real, imag, -1)
        for k in range(RADIX):
            ring[in_ring(unit, k, 0), :] = real[k]
            ring[in_ring(unit, k, 1), :] = imag[k]

    def backward(i, ax):
        values = jnp.concatenate(
            [ring[pl.ds(pl.multiple_of((l * RADIX + ax) * 128, 128), 128), :] for l in range(2)], axis=1
        )
        high, low = halves(values)
        total = dot(high, turned_ref[0]) + dot(high, turned_ref[1]) + dot(low, turned_ref[0])
        cosine, sine = total[:, :FOLD], total[:, FOLD:]
        first, second = [], []
        for h in range(2):
            re, im = slice(h * 64, h * 64 + 32), slice(h * 64 + 32, h * 64 + 64)
            first += [cosine[re] - sine[im], cosine[im] + sine[re]]
            second += [cosine[re] + sine[im], cosine[im] - sine[re]]
        base = pl.multiple_of((ax * (RADIX // 2) + i) * PAD, PAD)
        waves[pl.ds(base, FOLD), :] = jnp.concatenate(first, axis=0).T
        waves[pl.ds(base + FOLD, FOLD), :] = jnp.concatenate(second, axis=0).T

    slabs = RADIX // 2

    def first_slab(j, carry):
        forward(0, j)
        return carry

    def forward_slab(i, carry):
        for j in range(RADIX):
            forward_x(i - 1, j)
        for j in range(RADIX):
            forward(i, j)
        return carry

    lax.fori_loop(0, RADIX, first_slab, 0, unroll=8)
    lax.fori_loop(1, slabs, forward_slab, 0)
    for j in range(RADIX):
        forward_x(slabs - 1, j)

    def along_y(ax, carry):
        for l in range(2):
            lanes = pl.ds(l * 128, 128)
            for b in range(4):
                def at(k, c):
                    base = pl.multiple_of((l * COMBOS + ax * RADIX) * LANES, LANES)
                    return pl.ds(base + k * LANES + c * 32 + b * 8, 8)

                real = [waves[at(k, 0), :] for k in range(RADIX)]
                imag = [waves[at(k, 1), :] for k in range(RADIX)]
                real, imag = butterfly(real, imag, 1)
                local = [local_ref[ax * RADIX + k, :, lanes] for k in range(RADIX)]
                real = [value * local[k] for k, value in enumerate(real)]
                imag = [value * local[k] for k, value in enumerate(imag)]
                real, imag = butterfly(real, imag, -1)
                for k in range(RADIX):
                    columns[at(k, 0), :] = real[k]
                    columns[at(k, 1), :] = imag[k]
        return carry

    lax.fori_loop(0, RADIX, along_y, 0, unroll=UNROLL_Y)

    for j in range(RADIX):
        backward_x(0, j)

    def backward_slab(i, carry):
        for j in range(RADIX):
            backward(i - 1, j)
        for j in range(RADIX):
            backward_x(i, j)
        return carry

    def final_slab(j, carry):
        backward(slabs - 1, j)
        return carry

    lax.fori_loop(1, slabs, backward_slab, 0)
    lax.fori_loop(0, RADIX, final_slab, 0, unroll=8)
    staged[...] = jnp.zeros_like(staged)

    def gather(g):
        value = waves[pl.ds(row_ref[g], 1), :]
        pltpu.store(staged.at[pl.ds(source_ref[g], 1), :], value, mask=lane_half == half_ref[g])

    over_live(gather)

    def restore(quad, carry):
        base = pl.multiple_of(quad * 128, 128)
        block = staged[pl.ds(base, 128), :] + pltpu.roll(staged[pl.ds(rows + base, 128), :], 64, 1)
        block = block.T
        for pair in range(2):
            d = quad * 4 + pair * 2
            for c in range(2):
                for t in range(2):
                    line = (pair * 8 + c * 4 + t * 2) * 8
                    first, second = swap_halves(block[line : line + 8], block[line + 8 : line + 16])
                    at = (pl.ds(c * 8, 8), pl.ds(t * 128, 128))
                    out_ref[d, at[0], at[1]] = first
                    out_ref[d + 1, at[0], at[1]] = second
        return carry

    lax.fori_loop(0, devices // 4, restore, 0, unroll=4)


def on_grid(source, row, half, count, sticks, local):
    table = folded_table()
    turned = np.swapaxes(table, 1, 2)
    rows = sticks.shape[0] * 32
    smem = pl.BlockSpec(memory_space=pltpu.SMEM)
    vmem = pl.BlockSpec(memory_space=pltpu.VMEM)
    return pl.pallas_call(
        grid_kernel,
        out_shape=jax.ShapeDtypeStruct(sticks.shape, jnp.float32),
        in_specs=[smem] * 4 + [vmem] * 4,
        out_specs=vmem,
        scratch_shapes=[
            pltpu.VMEM((COMBOS // 2 * PAD, 128), jnp.float32),
            pltpu.VMEM((COMBOS // 2 * PAD, 128), jnp.float32),
            pltpu.VMEM((2 * RADIX * 128, 128), jnp.float32),
            pltpu.VMEM((2 * rows, 128), jnp.float32),
        ],
        compiler_params=pltpu.CompilerParams(vmem_limit_bytes=60 * 2**20),
    )(source, row, half, count, sticks, local, jnp.asarray(table), jnp.asarray(turned))


class Layout:
    def __init__(self, tg_size, fft_size, plane_slots):
        self.tg_size, self.fft_size, self.plane_slots = tg_size, fft_size, plane_slots
        self.devices = tg_size * fft_size
        self.chunk = -(-plane_slots // tg_size)
        self.starts = [t * self.chunk // SLOTS * SLOTS for t in range(tg_size)]


def greet(n, fft_size, me):
    barrier = pltpu.get_barrier_semaphore()

    def signal(i, carry):
        other = lax.rem(me + i, n)
        pl.semaphore_signal(
            barrier, inc=1, device_id=(other // fft_size, lax.rem(other, fft_size)), device_id_type=MESH
        )
        return carry

    lax.fori_loop(1, n, signal, 0)
    return lambda: pl.semaphore_wait(barrier, n - 1)


def exchange(n, fft_size, me, source, target, send_sem, recv_sem):
    def copy(i):
        other = lax.rem(me + i, n)
        return pltpu.make_async_remote_copy(
            src_ref=source.at[other], dst_ref=target.at[me], send_sem=send_sem.at[i], recv_sem=recv_sem.at[i],
            device_id=(other // fft_size, lax.rem(other, fft_size)), device_id_type=MESH,
        )

    def start(i, carry):
        copy(i).start()
        return carry

    def wait(i, carry):
        copy(i).wait()
        return carry

    own = pltpu.make_async_copy(source.at[me], target.at[me], send_sem.at[0])

    def begin():
        lax.fori_loop(1, n, start, 0)
        own.start()

    def finish():
        own.wait()
        lax.fori_loop(1, n, wait, 0)

    return begin, finish


def plane_tables(layout, owner_ref, table_ref, first):
    owner = jnp.broadcast_to(owner_ref[...], (PAD, PAD)).astype(jnp.float32)
    index = lax.broadcasted_iota(jnp.int32, (PAD, PAD), 0)
    same = (owner == owner.T) & (index < lax.broadcasted_iota(jnp.int32, (PAD, PAD), 1))
    rank = jnp.sum(jnp.where(same, 1.0, 0.0), axis=0, keepdims=True)
    group = jnp.zeros_like(rank)
    offset = jnp.zeros_like(rank)
    for t in range(1, layout.tg_size):
        beyond = rank >= float(t * layout.chunk)
        group = jnp.where(beyond, float(t), group)
        offset = jnp.where(beyond, float(layout.starts[t]), offset)
    row = (group * layout.fft_size + owner[:1]) * SLOTS + rank - offset
    pick = jnp.where(index.astype(jnp.float32) + float(first) == row, 1.0, 0.0).astype(jnp.bfloat16)
    return dot(pick, table_ref[0]).astype(jnp.bfloat16), dot(pick, table_ref[1]).astype(jnp.bfloat16)


def lift_kernel(
    layout, coeffs_ref, owner_ref, potential_ref, table_ref, order_ref, out_ref, local_ref,
    parts, slab, lines, spread, send_sem, recv_sem, slab_sem,
):
    n, fft_size = layout.devices, layout.fft_size
    tg = lax.axis_index("tg")
    me = tg * fft_size + lax.axis_index("fft")
    greeted = greet(n, fft_size, me)

    slabs = []
    for t in range(layout.tg_size):
        start = layout.starts[t]
        count = min(SLOTS, layout.plane_slots - start)
        slabs.append((t, count, pltpu.make_async_copy(
            potential_ref.at[pl.ds(start, count), :], slab.at[pl.ds(0, count), :], slab_sem
        )))
    for t, count, copy in slabs:
        @pl.when(tg == t)
        def _():
            if count < SLOTS:
                slab[...] = jnp.zeros_like(slab)
            copy.start()

    bands, _, sticks, _ = coeffs_ref.shape
    real = halves(coeffs_ref[:, 0].reshape(bands * sticks, NZ))
    imag = halves(coeffs_ref[:, 1].reshape(bands * sticks, NZ))

    def three(high, low, values):
        return dot_last(high, values[0]) + dot_last(low, values[0]) + dot_last(high, values[1])

    per = PAD // SLOTS
    for first in range(0, n, per):
        high, low = plane_tables(layout, owner_ref, table_ref, first * SLOTS)
        cos_high, cos_low = high[:, :NZ], low[:, :NZ]
        sin_high, sin_low = high[:, PAD : PAD + NZ], low[:, PAD : PAD + NZ]
        up_real = three(cos_high, cos_low, real) - three(sin_high, sin_low, imag)
        up_imag = three(sin_high, sin_low, real) + three(cos_high, cos_low, imag)
        parts[first : first + per, :SLOTS] = up_real.reshape(per, SLOTS, bands * sticks)
        parts[first : first + per, SLOTS:] = up_imag.reshape(per, SLOTS, bands * sticks)

    begin, finish = exchange(n, fft_size, me, parts, out_ref, send_sem, recv_sem)
    greeted()
    begin()

    for t, count, copy in slabs:
        @pl.when(tg == t)
        def _():
            copy.wait()

    lines[:, NY:] = jnp.zeros((NX * SLOTS, PAD - NY), jnp.float32)

    def cut(q, carry):
        wide = slab[:, pl.ds(pl.multiple_of(q * 8 * NY, 128), 8 * NY)]
        for r in range(8):
            lines[pl.ds(pl.multiple_of(q * 8 * SLOTS, 8 * SLOTS) + r * SLOTS, SLOTS), :NY] = wide[:, r * NY : (r + 1) * NY]
        return carry

    lax.fori_loop(0, NX // 8, cut, 0)
    order = order_ref[...]

    def reorder(i, carry):
        at = pl.ds(pl.multiple_of(i * 128, 128), 128)
        values = lines[at, :]
        high, low = halves(values)
        rest = (values - high.astype(jnp.float32) - low.astype(jnp.float32)).astype(jnp.bfloat16)
        spread[at, :] = dot(high, order) + dot(low, order) + dot(rest, order)
        return carry

    lax.fori_loop(0, NX * SLOTS // 128, reorder, 0)
    lane_block = lax.broadcasted_iota(jnp.int32, (SLOTS, 128), 1) // RADIX

    def regroup(nx, carry):
        tiles = []
        for mx in range(ODD):
            x = lax.rem(nx * ODD + mx * RADIX, NX)
            at = pl.ds(pl.multiple_of(x * SLOTS, SLOTS), SLOTS)
            tiles.append([spread[at, :128], spread[at, 128:]])
        tiles.append([jnp.zeros((SLOTS, 128), jnp.float32)] * 2)
        tiles = [[tiles[m % 8 + 8 * (h % 2)][m // 8] for h in range(2)] for m in range(16)]
        for bit in (4, 2, 1):
            shift = bit * RADIX
            clear = lane_block % (2 * bit) < bit
            fresh = [[None, None] for _ in range(16)]
            for m in range(16):
                if m & bit:
                    continue
                for h in range(2):
                    a, b = tiles[m][h], tiles[m | bit][h]
                    fresh[m][h] = jnp.where(clear, a, pltpu.roll(b, shift, 1))
                    fresh[m | bit][h] = jnp.where(clear, pltpu.roll(a, 128 - shift, 1), b)
            tiles = fresh
        for ny in range(16):
            local_ref[nx * RADIX + ny, :, :128] = tiles[ny][0]
            local_ref[nx * RADIX + ny, :, 128:] = tiles[ny][1]
        return carry

    lax.fori_loop(0, RADIX, regroup, 0)
    finish()


def lift(layout, coeffs, owner, potential):
    bands, _, sticks, _ = coeffs.shape
    n = layout.devices
    hbm = pl.BlockSpec(memory_space=pl.ANY)
    vmem = pl.BlockSpec(memory_space=pltpu.VMEM)
    return pl.pallas_call(
        functools.partial(lift_kernel, layout),
        out_shape=(
            jax.ShapeDtypeStruct((n, 2 * SLOTS, bands * sticks), jnp.float32),
            jax.ShapeDtypeStruct((COMBOS, SLOTS, PAD), jnp.float32),
        ),
        in_specs=[vmem, vmem, hbm, vmem, vmem],
        out_specs=(hbm, vmem),
        scratch_shapes=[
            pltpu.VMEM((n, 2 * SLOTS, bands * sticks), jnp.float32),
            pltpu.VMEM((SLOTS, NX * NY), jnp.float32),
            pltpu.VMEM((NX * SLOTS, PAD), jnp.float32),
            pltpu.VMEM((NX * SLOTS, PAD), jnp.float32),
            pltpu.SemaphoreType.DMA((n,)),
            pltpu.SemaphoreType.DMA((n,)),
            pltpu.SemaphoreType.DMA,
        ],
        compiler_params=pltpu.CompilerParams(
            collective_id=0, has_side_effects=True, vmem_limit_bytes=48 * 2**20
        ),
    )(coeffs, owner, potential, jnp.asarray(z_table()), jnp.asarray(y_order()))


def back_kernel(layout, worked_ref, owner_ref, count_ref, table_ref, out_ref, received, send_sem, recv_sem):
    n, fft_size = layout.devices, layout.fft_size
    me = lax.axis_index("tg") * fft_size + lax.axis_index("fft")
    begin, finish = exchange(n, fft_size, me, worked_ref, received, send_sem, recv_sem)
    greet(n, fft_size, me)()
    begin()
    per = PAD // SLOTS
    tables = [plane_tables(layout, owner_ref, table_ref, first * SLOTS) for first in range(0, n, per)]
    finish()

    bands, _, sticks, _ = out_ref.shape
    out_real = jnp.zeros((bands * sticks, PAD), jnp.float32)
    out_imag = jnp.zeros((bands * sticks, PAD), jnp.float32)

    def three(values, high, low):
        return dot(values[0], high) + dot(values[0], low) + dot(values[1], high)

    for index, first in enumerate(range(0, n, per)):
        high, low = tables[index]
        real = halves(received[first : first + per, :SLOTS].reshape(PAD, bands * sticks).T)
        imag = halves(received[first : first + per, SLOTS:].reshape(PAD, bands * sticks).T)
        cos_high, cos_low = high[:, :PAD], low[:, :PAD]
        sin_high, sin_low = high[:, PAD:], low[:, PAD:]
        out_real += three(real, cos_high, cos_low) + three(imag, sin_high, sin_low)
        out_imag += three(imag, cos_high, cos_low) - three(real, sin_high, sin_low)
    live = lax.broadcasted_iota(jnp.int32, (bands, sticks, NZ), 1) < count_ref[me]
    out_ref[:, 0] = jnp.where(live, out_real[:, :NZ].reshape(bands, sticks, NZ), 0.0)
    out_ref[:, 1] = jnp.where(live, out_imag[:, :NZ].reshape(bands, sticks, NZ), 0.0)


def lower(layout, worked, owner, count, shape):
    n = layout.devices
    hbm = pl.BlockSpec(memory_space=pl.ANY)
    vmem = pl.BlockSpec(memory_space=pltpu.VMEM)
    return pl.pallas_call(
        functools.partial(back_kernel, layout),
        out_shape=jax.ShapeDtypeStruct(shape, jnp.float32),
        in_specs=[hbm, vmem, pl.BlockSpec(memory_space=pltpu.SMEM), vmem],
        out_specs=vmem,
        scratch_shapes=[
            pltpu.VMEM(worked.shape, jnp.float32),
            pltpu.SemaphoreType.DMA((n,)),
            pltpu.SemaphoreType.DMA((n,)),
        ],
        compiler_params=pltpu.CompilerParams(
            collective_id=1, has_side_effects=True, vmem_limit_bytes=48 * 2**20
        ),
    )(worked, owner, count, jnp.asarray(z_table()))


def stick_places(stick_count, stick_column, slot_count, devices):
    slot = jnp.arange(slot_count, dtype=jnp.int32)
    live = (slot[None, :] < stick_count[:, None]).reshape(-1)
    x, y = stick_column // NY, stick_column % NY
    combo = x % RADIX * RADIX + y % RADIX
    bx, by = x % ODD, y % ODD
    negative = (bx > ODD // 2) | ((bx == 0) & (by > ODD // 2))
    bx = jnp.where(negative & (bx > 0), ODD - bx, bx)
    by = jnp.where(negative & (by > 0), ODD - by, by)
    place = jnp.where(bx == 0, by, ODD // 2 + 1 + (bx - 1) * ODD + by) + jnp.where(negative, FOLD, 0)
    row = jnp.where(live, combo // 2 * PAD + place, FOLD - 1)
    half = combo % 2
    glob = jnp.arange(devices * slot_count, dtype=jnp.int32)
    device, within = glob // slot_count, glob % slot_count
    source = device // 4 * 128 + device % 2 * 64 + within
    source = source + jnp.where(device // 2 % 2 != half, devices * slot_count // 2, 0)
    return source, row, half


def per_device(coeffs, stick_count, stick_column, plane_owner, potential):
    layout = Layout(lax.axis_size("tg"), lax.axis_size("fft"), potential.shape[0])
    slot_count = coeffs.shape[3]
    turned = jnp.swapaxes(coeffs, 2, 3)
    owner = jnp.pad(plane_owner, (0, PAD - NZ), constant_values=layout.fft_size * 2).reshape(1, PAD)
    sticks, local = lift(layout, turned, owner, potential)
    source, row, half = stick_places(stick_count, stick_column, slot_count, layout.devices)
    worked = on_grid(source, row, half, stick_count, sticks, local)
    applied = lower(layout, worked, owner, stick_count, turned.shape)
    return jnp.swapaxes(applied, 2, 3)


def solution(mesh):
    in_specs = (P(None, None, None, ("tg", "fft")), P(), P(), P(), P("fft", None))
    out_specs = P(None, None, None, ("tg", "fft"))
    return jax.shard_map(
        per_device, mesh=mesh, in_specs=in_specs, out_specs=out_specs, check_vma=False
    )
```

```python
import functools
import math

import jax
import jax.numpy as jnp
import ml_dtypes
import numpy as np
from jax import lax
from jax.experimental import pallas as pl
from jax.experimental.pallas import tpu as pltpu
from jax.sharding import PartitionSpec as P

NX = 240
NY = 240
NZ = 240
PAD = 256
FOLD = 128
LANES = 64
RADIX = 16
ODD = 15
COMBOS = RADIX * RADIX
SLOTS = 8
GROUP = 8
UNROLL_Y = 2
MESH = pl.DeviceIdType.MESH


def split_table(table):
    table = table.astype(np.float32)
    high = table.astype(ml_dtypes.bfloat16)
    low = (table - high.astype(np.float32)).astype(ml_dtypes.bfloat16)
    return np.stack([high, low])


def z_table():
    indices = np.arange(NZ)
    angles = (indices[:, None] * indices[None, :] % NZ) * (2.0 * math.pi / NZ)
    table = np.zeros((PAD, 2 * PAD))
    table[:NZ, :NZ] = np.cos(angles) / math.sqrt(NZ)
    table[:NZ, PAD : PAD + NZ] = np.sin(angles) / math.sqrt(NZ)
    return split_table(table)


def folded_table():
    first = np.arange(ODD)
    table = np.zeros((PAD, PAD))
    for bx in range(ODD // 2 + 1):
        for by in range(ODD if bx else ODD // 2 + 1):
            i = ODD // 2 + 1 + (bx - 1) * ODD + by if bx else by
            angles = ((bx * first[:, None] + by * first[None, :]) % ODD) * (2.0 * math.pi / ODD)
            wide = np.zeros((2, RADIX, RADIX))
            wide[0, :ODD, :ODD] = np.cos(angles)
            wide[1, :ODD, :ODD] = -np.sin(angles)
            table[i] = wide[0].reshape(-1) / NX
            table[FOLD + i] = wide[1].reshape(-1) / NX
    return split_table(table)


def y_order():
    order = np.zeros((PAD, PAD), np.float32)
    y = np.arange(NY)
    order[y, (-y) % RADIX * RADIX + y % ODD] = 1.0
    return order.astype(ml_dtypes.bfloat16)


def halves(values):
    high = values.astype(jnp.bfloat16)
    low = (values - high.astype(jnp.float32)).astype(jnp.bfloat16)
    return high, low


def dot(a, b):
    return jnp.dot(a, b, preferred_element_type=jnp.float32)


def dot_last(a, b):
    return lax.dot_general(a, b, (((1,), (1,)), ((), ())), preferred_element_type=jnp.float32)


def butterfly(real, imag, sign):
    def four(xs):
        (ar, ai), (br, bi), (cr, ci), (dr, di) = xs
        er, ei, fr, fi = ar + cr, ai + ci, ar - cr, ai - ci
        gr, gi, hr, hi = br + dr, bi + di, br - dr, bi - di
        if sign > 0:
            return [(er + gr, ei + gi), (fr - hi, fi + hr), (er - gr, ei - gi), (fr + hi, fi - hr)]
        return [(er + gr, ei + gi), (fr + hi, fi - hr), (er - gr, ei - gi), (fr - hi, fi + hr)]

    def turn(x, power):
        r, i = x
        root = math.sqrt(0.5)
        if power == 0:
            return x
        if power == 4:
            return (-i, r) if sign > 0 else (i, -r)
        if power == 2:
            return ((r - i) * root, (r + i) * root) if sign > 0 else ((r + i) * root, (i - r) * root)
        if power == 6:
            return ((r + i) * -root, (r - i) * root) if sign > 0 else ((i - r) * root, (r + i) * -root)
        c = math.cos(2 * math.pi * power / 16)
        s = math.sin(2 * math.pi * power / 16) * sign
        return r * c - i * s, r * s + i * c

    inner = [four([(real[4 * n1 + n2], imag[4 * n1 + n2]) for n1 in range(4)]) for n2 in range(4)]
    out_real, out_imag = [None] * 16, [None] * 16
    for k1 in range(4):
        outer = four([turn(inner[n2][k1], n2 * k1) for n2 in range(4)])
        for k2 in range(4):
            out_real[k1 + 4 * k2], out_imag[k1 + 4 * k2] = outer[k2]
    return out_real, out_imag


def swap_halves(first, second):
    lower = lax.broadcasted_iota(jnp.int32, first.shape, first.ndim - 1) < 64
    first_turned = pltpu.roll(first, 64, first.ndim - 1)
    second_turned = pltpu.roll(second, 64, second.ndim - 1)
    return jnp.where(lower, first, second_turned), jnp.where(lower, first_turned, second)


def grid_kernel(
    source_ref, row_ref, half_ref, count_ref, sticks_hbm, local_hbm, table_hbm, turned_hbm, out_ref,
    columns, waves, ring, staged, local_ref, table_ref, turned_ref, load_sem,
):
    loads = [
        pltpu.make_async_copy(source, target, load_sem.at[i])
        for i, (source, target) in enumerate(
            [(sticks_hbm, out_ref), (table_hbm, table_ref), (local_hbm, local_ref), (turned_hbm, turned_ref)]
        )
    ]
    for load in loads:
        load.start()
    devices = out_ref.shape[0]
    rows = devices * 32
    lane_half = lax.broadcasted_iota(jnp.int32, (1, 128), 1) // 64

    def clear(i, carry):
        columns[pl.ds(pl.multiple_of(i * PAD, PAD), PAD), :] = jnp.zeros((PAD, 128), jnp.float32)
        return carry

    lax.fori_loop(0, COMBOS // 2, clear, 0)
    loads[0].wait()

    def arrange(quad, carry):
        lines = [None] * 16
        for pair in range(2):
            d = quad * 4 + pair * 2
            for c in range(2):
                for t in range(2):
                    at = (pl.ds(c * 8, 8), pl.ds(t * 128, 128))
                    even, odd = swap_halves(out_ref[d, at[0], at[1]], out_ref[d + 1, at[0], at[1]])
                    lines[pair * 8 + c * 4 + t * 2] = even
                    lines[pair * 8 + c * 4 + t * 2 + 1] = odd
        block = jnp.concatenate(lines, axis=0).T
        base = pl.multiple_of(quad * 128, 128)
        staged[pl.ds(base, 128), :] = block
        staged[pl.ds(rows + base, 128), :] = pltpu.roll(block, 64, 1)
        return carry

    lax.fori_loop(0, devices // 4, arrange, 0, unroll=4)

    def over_live(work):
        def per_device(d, carry):
            def per_group(i, inner):
                for j in range(GROUP):
                    work(d * 64 + i * GROUP + j)
                return inner

            return lax.fori_loop(0, (count_ref[d] + GROUP - 1) // GROUP, per_group, carry)

        lax.fori_loop(0, devices, per_device, 0)

    def scatter(g):
        value = staged[pl.ds(source_ref[g], 1), :]
        pltpu.store(columns.at[pl.ds(row_ref[g], 1), :], value, mask=lane_half == half_ref[g])

    over_live(scatter)

    def forward(i, ax):
        base = pl.multiple_of((ax * (RADIX // 2) + i) * PAD, PAD)
        low_half = columns[pl.ds(base, FOLD), :].T
        high_half = columns[pl.ds(base + FOLD, FOLD), :].T
        odd = []
        for h in range(2):
            re, im = slice(h * 64, h * 64 + 32), slice(h * 64 + 32, h * 64 + 64)
            odd += [low_half[im] - high_half[im], high_half[re] - low_half[re]]
        values = jnp.concatenate([low_half + high_half, jnp.concatenate(odd, axis=0)], axis=1)
        high, low = halves(values)
        total = dot(high, table_ref[0]) + dot(high, table_ref[1]) + dot(low, table_ref[0])
        for l in range(2):
            ring[pl.ds(pl.multiple_of((l * RADIX + ax) * 128, 128), 128), :] = total[:, l * 128 : (l + 1) * 128]

    def in_ring(unit, k, c):
        h, b, l = unit // 8, unit // 2 % 4, unit % 2
        return pl.ds((l * RADIX + k) * 128 + h * 64 + c * 32 + b * 8, 8)

    def in_grid(i, unit, k, c):
        h, b, l = unit // 8, unit // 2 % 4, unit % 2
        base = pl.multiple_of(2 * i * LANES, 128)
        return pl.ds(base + (l * COMBOS + k * RADIX + h) * LANES + c * 32 + b * 8, 8)

    def forward_x(i, unit):
        real = [ring[in_ring(unit, k, 0), :] for k in range(RADIX)]
        imag = [ring[in_ring(unit, k, 1), :] for k in range(RADIX)]
        real, imag = butterfly(real, imag, 1)
        for k in range(RADIX):
            waves[in_grid(i, unit, k, 0), :] = real[k]
            waves[in_grid(i, unit, k, 1), :] = imag[k]

    def backward_x(i, unit):
        real = [columns[in_grid(i, unit, k, 0), :] for k in range(RADIX)]
        imag = [columns[in_grid(i, unit, k, 1), :] for k in range(RADIX)]
        real, imag = butterfly(real, imag, -1)
        for k in range(RADIX):
            ring[in_ring(unit, k, 0), :] = real[k]
            ring[in_ring(unit, k, 1), :] = imag[k]

    def backward(i, ax):
        values = jnp.concatenate(
            [ring[pl.ds(pl.multiple_of((l * RADIX + ax) * 128, 128), 128), :] for l in range(2)], axis=1
        )
        high, low = halves(values)
        total = dot(high, turned_ref[0]) + dot(high, turned_ref[1]) + dot(low, turned_ref[0])
        cosine, sine = total[:, :FOLD], total[:, FOLD:]
        first, second = [], []
        for h in range(2):
            re, im = slice(h * 64, h * 64 + 32), slice(h * 64 + 32, h * 64 + 64)
            first += [cosine[re] - sine[im], cosine[im] + sine[re]]
            second += [cosine[re] + sine[im], cosine[im] - sine[re]]
        base = pl.multiple_of((ax * (RADIX // 2) + i) * PAD, PAD)
        waves[pl.ds(base, FOLD), :] = jnp.concatenate(first, axis=0).T
        waves[pl.ds(base + FOLD, FOLD), :] = jnp.concatenate(second, axis=0).T

    slabs = RADIX // 2

    def first_slab(j, carry):
        forward(0, j)
        return carry

    def forward_slab(i, carry):
        for j in range(RADIX):
            forward_x(i - 1, j)
        for j in range(RADIX):
            forward(i, j)
        return carry

    loads[1].wait()
    lax.fori_loop(0, RADIX, first_slab, 0, unroll=8)
    lax.fori_loop(1, slabs, forward_slab, 0)
    for j in range(RADIX):
        forward_x(slabs - 1, j)

    def along_y(ax, carry):
        for l in range(2):
            lanes = pl.ds(l * 128, 128)
            for b in range(4):
                def at(k, c):
                    base = pl.multiple_of((l * COMBOS + ax * RADIX) * LANES, LANES)
                    return pl.ds(base + k * LANES + c * 32 + b * 8, 8)

                real = [waves[at(k, 0), :] for k in range(RADIX)]
                imag = [waves[at(k, 1), :] for k in range(RADIX)]
                real, imag = butterfly(real, imag, 1)
                local = [local_ref[ax * RADIX + k, :, lanes] for k in range(RADIX)]
                real = [value * local[k] for k, value in enumerate(real)]
                imag = [value * local[k] for k, value in enumerate(imag)]
                real, imag = butterfly(real, imag, -1)
                for k in range(RADIX):
                    columns[at(k, 0), :] = real[k]
                    columns[at(k, 1), :] = imag[k]
        return carry

    loads[2].wait()
    loads[3].wait()
    lax.fori_loop(0, RADIX, along_y, 0, unroll=UNROLL_Y)

    for j in range(RADIX):
        backward_x(0, j)

    def backward_slab(i, carry):
        for j in range(RADIX):
            backward(i - 1, j)
        for j in range(RADIX):
            backward_x(i, j)
        return carry

    def final_slab(j, carry):
        backward(slabs - 1, j)
        return carry

    lax.fori_loop(1, slabs, backward_slab, 0)
    lax.fori_loop(0, RADIX, final_slab, 0, unroll=8)
    staged[...] = jnp.zeros_like(staged)

    def gather(g):
        value = waves[pl.ds(row_ref[g], 1), :]
        pltpu.store(staged.at[pl.ds(source_ref[g], 1), :], value, mask=lane_half == half_ref[g])

    over_live(gather)

    def restore(quad, carry):
        base = pl.multiple_of(quad * 128, 128)
        block = staged[pl.ds(base, 128), :] + pltpu.roll(staged[pl.ds(rows + base, 128), :], 64, 1)
        block = block.T
        for pair in range(2):
            d = quad * 4 + pair * 2
            for c in range(2):
                for t in range(2):
                    line = (pair * 8 + c * 4 + t * 2) * 8
                    first, second = swap_halves(block[line : line + 8], block[line + 8 : line + 16])
                    at = (pl.ds(c * 8, 8), pl.ds(t * 128, 128))
                    out_ref[d, at[0], at[1]] = first
                    out_ref[d + 1, at[0], at[1]] = second
        return carry

    lax.fori_loop(0, devices // 4, restore, 0, unroll=4)


def on_grid(source, row, half, count, sticks, local):
    table = folded_table()
    turned = np.swapaxes(table, 1, 2)
    rows = sticks.shape[0] * 32
    smem = pl.BlockSpec(memory_space=pltpu.SMEM)
    vmem = pl.BlockSpec(memory_space=pltpu.VMEM)
    return pl.pallas_call(
        grid_kernel,
        out_shape=jax.ShapeDtypeStruct(sticks.shape, jnp.float32),
        in_specs=[smem] * 4 + [pl.BlockSpec(memory_space=pl.ANY)] * 4,
        out_specs=vmem,
        scratch_shapes=[
            pltpu.VMEM((COMBOS // 2 * PAD, 128), jnp.float32),
            pltpu.VMEM((COMBOS // 2 * PAD, 128), jnp.float32),
            pltpu.VMEM((2 * RADIX * 128, 128), jnp.float32),
            pltpu.VMEM((2 * rows, 128), jnp.float32),
            pltpu.VMEM(local.shape, jnp.float32),
            pltpu.VMEM(table.shape, jnp.bfloat16),
            pltpu.VMEM(table.shape, jnp.bfloat16),
            pltpu.SemaphoreType.DMA((4,)),
        ],
        compiler_params=pltpu.CompilerParams(vmem_limit_bytes=60 * 2**20),
    )(source, row, half, count, sticks, local, jnp.asarray(table), jnp.asarray(turned))


class Layout:
    def __init__(self, tg_size, fft_size, plane_slots):
        self.tg_size, self.fft_size, self.plane_slots = tg_size, fft_size, plane_slots
        self.devices = tg_size * fft_size
        self.chunk = -(-plane_slots // tg_size)
        self.starts = [t * self.chunk // SLOTS * SLOTS for t in range(tg_size)]


def greet(n, fft_size, me):
    barrier = pltpu.get_barrier_semaphore()

    def signal(i, carry):
        other = lax.rem(me + i, n)
        pl.semaphore_signal(
            barrier, inc=1, device_id=(other // fft_size, lax.rem(other, fft_size)), device_id_type=MESH
        )
        return carry

    lax.fori_loop(1, n, signal, 0)
    return lambda: pl.semaphore_wait(barrier, n - 1)


def exchange(n, fft_size, me, source, target, send_sem, recv_sem):
    def copy(i):
        other = lax.rem(me + i, n)
        return pltpu.make_async_remote_copy(
            src_ref=source.at[other], dst_ref=target.at[me], send_sem=send_sem.at[i], recv_sem=recv_sem.at[i],
            device_id=(other // fft_size, lax.rem(other, fft_size)), device_id_type=MESH,
        )

    def start(i, carry):
        copy(i).start()
        return carry

    def wait(i, carry):
        copy(i).wait()
        return carry

    own = pltpu.make_async_copy(source.at[me], target.at[me], send_sem.at[0])

    def begin():
        lax.fori_loop(1, n, start, 0)
        own.start()

    def finish():
        own.wait()
        lax.fori_loop(1, n, wait, 0)

    return begin, finish


def plane_tables(layout, owner_ref, table_ref, first):
    outside = jnp.full((1, PAD - NZ), 2 * layout.fft_size, jnp.int32)
    owner = jnp.concatenate([owner_ref[...], outside], axis=1).astype(jnp.float32)
    owner = jnp.broadcast_to(owner, (PAD, PAD))
    index = lax.broadcasted_iota(jnp.int32, (PAD, PAD), 0)
    same = (owner == owner.T) & (index < lax.broadcasted_iota(jnp.int32, (PAD, PAD), 1))
    rank = jnp.sum(jnp.where(same, 1.0, 0.0), axis=0, keepdims=True)
    group = jnp.zeros_like(rank)
    offset = jnp.zeros_like(rank)
    for t in range(1, layout.tg_size):
        beyond = rank >= float(t * layout.chunk)
        group = jnp.where(beyond, float(t), group)
        offset = jnp.where(beyond, float(layout.starts[t]), offset)
    row = (group * layout.fft_size + owner[:1]) * SLOTS + rank - offset
    pick = jnp.where(index.astype(jnp.float32) + float(first) == row, 1.0, 0.0).astype(jnp.bfloat16)
    return dot(pick, table_ref[0]).astype(jnp.bfloat16), dot(pick, table_ref[1]).astype(jnp.bfloat16)


def divided(value, divisor):
    quotient = jnp.floor((value + 0.5) * (1.0 / divisor))
    return quotient, value - quotient * divisor


def stick_places(count_ref, column_ref, source_ref, row_ref, half_ref):
    rows = column_ref.shape[0]
    lane = lax.broadcasted_iota(jnp.int32, (8, 128), 1)
    sublane = lax.broadcasted_iota(jnp.int32, (8, 128), 0)
    within = lane % 64
    middle, last = float(ODD // 2), float(FOLD - 1)

    def step(i, carry):
        at = pl.ds(pl.multiple_of(i * 8, 8), 8)
        count = jnp.zeros((8, 128), jnp.int32)
        for r in range(8):
            for h in range(2):
                count = jnp.where((sublane == r) & (lane // 64 == h), count_ref[i * 16 + 2 * r + h], count)
        x, y = divided(column_ref[at, :].astype(jnp.float32), float(NY))
        ax, ay = divided(x, float(RADIX))[1], divided(y, float(RADIX))[1]
        bx, by = divided(x, float(ODD))[1], divided(y, float(ODD))[1]
        negative = (bx > middle) | ((bx == 0.0) & (by > middle))
        bx = jnp.where(negative & (bx > 0.0), ODD - bx, bx)
        by = jnp.where(negative & (by > 0.0), ODD - by, by)
        place = jnp.where(bx == 0.0, by, middle + 1.0 + (bx - 1.0) * ODD + by)
        place = place + jnp.where(negative, float(FOLD), 0.0)
        pair, half = divided(ax * RADIX + ay, 2.0)
        row_ref[at, :] = jnp.where(within < count, pair * PAD + place, last).astype(jnp.int32)
        half = half.astype(jnp.int32)
        half_ref[at, :] = half
        slot_row = i * 8 + sublane
        source = slot_row // 2 * 128 + lane
        source_ref[at, :] = source + jnp.where(slot_row % 2 != half, rows * 64, 0)
        return carry

    lax.fori_loop(0, rows // 8, step, 0)


def lift_kernel(
    layout, coeffs_hbm, owner_ref, count_ref, column_ref, potential_ref, table_hbm, order_hbm,
    out_ref, local_ref, source_ref, row_ref, half_ref,
    parts, slab, lines, spread, coeffs_ref, table_ref, order_ref, send_sem, recv_sem, slab_sem, load_sem,
):
    n, fft_size = layout.devices, layout.fft_size
    tg = lax.axis_index("tg")
    me = tg * fft_size + lax.axis_index("fft")
    loads = [
        pltpu.make_async_copy(source, target, load_sem.at[i])
        for i, (source, target) in enumerate(
            [(coeffs_hbm, coeffs_ref), (table_hbm, table_ref), (order_hbm, order_ref)]
        )
    ]
    for load in loads:
        load.start()
    greeted = greet(n, fft_size, me)

    slabs = []
    for t in range(layout.tg_size):
        start = layout.starts[t]
        count = min(SLOTS, layout.plane_slots - start)
        slabs.append((t, count, pltpu.make_async_copy(
            potential_ref.at[pl.ds(start, count), :], slab.at[pl.ds(0, count), :], slab_sem
        )))
    for t, count, copy in slabs:
        @pl.when(tg == t)
        def _():
            if count < SLOTS:
                slab[...] = jnp.zeros_like(slab)
            copy.start()

    loads[0].wait()
    loads[1].wait()
    bands, _, sticks, _ = coeffs_ref.shape
    real = halves(coeffs_ref[:, 0].reshape(bands * sticks, NZ))
    imag = halves(coeffs_ref[:, 1].reshape(bands * sticks, NZ))

    def three(high, low, values):
        return dot_last(high, values[0]) + dot_last(low, values[0]) + dot_last(high, values[1])

    per = PAD // SLOTS
    for first in range(0, n, per):
        high, low = plane_tables(layout, owner_ref, table_ref, first * SLOTS)
        cos_high, cos_low = high[:, :NZ], low[:, :NZ]
        sin_high, sin_low = high[:, PAD : PAD + NZ], low[:, PAD : PAD + NZ]
        up_real = three(cos_high, cos_low, real) - three(sin_high, sin_low, imag)
        up_imag = three(sin_high, sin_low, real) + three(cos_high, cos_low, imag)
        parts[first : first + per, :SLOTS] = up_real.reshape(per, SLOTS, bands * sticks)
        parts[first : first + per, SLOTS:] = up_imag.reshape(per, SLOTS, bands * sticks)

    begin, finish = exchange(n, fft_size, me, parts, out_ref, send_sem, recv_sem)
    greeted()
    begin()

    stick_places(count_ref, column_ref, source_ref, row_ref, half_ref)
    loads[2].wait()
    for t, count, copy in slabs:
        @pl.when(tg == t)
        def _():
            copy.wait()

    lines[:, NY:] = jnp.zeros((NX * SLOTS, PAD - NY), jnp.float32)

    def cut(q, carry):
        wide = slab[:, pl.ds(pl.multiple_of(q * 8 * NY, 128), 8 * NY)]
        for r in range(8):
            lines[pl.ds(pl.multiple_of(q * 8 * SLOTS, 8 * SLOTS) + r * SLOTS, SLOTS), :NY] = wide[:, r * NY : (r + 1) * NY]
        return carry

    lax.fori_loop(0, NX // 8, cut, 0)
    order = order_ref[...]

    def reorder(i, carry):
        at = pl.ds(pl.multiple_of(i * 128, 128), 128)
        values = lines[at, :]
        high, low = halves(values)
        rest = (values - high.astype(jnp.float32) - low.astype(jnp.float32)).astype(jnp.bfloat16)
        spread[at, :] = dot(high, order) + dot(low, order) + dot(rest, order)
        return carry

    lax.fori_loop(0, NX * SLOTS // 128, reorder, 0)
    lane_block = lax.broadcasted_iota(jnp.int32, (SLOTS, 128), 1) // RADIX

    def regroup(nx, carry):
        tiles = []
        for mx in range(ODD):
            x = lax.rem(nx * ODD + mx * RADIX, NX)
            at = pl.ds(pl.multiple_of(x * SLOTS, SLOTS), SLOTS)
            tiles.append([spread[at, :128], spread[at, 128:]])
        tiles.append([jnp.zeros((SLOTS, 128), jnp.float32)] * 2)
        tiles = [[tiles[m % 8 + 8 * (h % 2)][m // 8] for h in range(2)] for m in range(16)]
        for bit in (4, 2, 1):
            shift = bit * RADIX
            clear = lane_block % (2 * bit) < bit
            fresh = [[None, None] for _ in range(16)]
            for m in range(16):
                if m & bit:
                    continue
                for h in range(2):
                    a, b = tiles[m][h], tiles[m | bit][h]
                    fresh[m][h] = jnp.where(clear, a, pltpu.roll(b, shift, 1))
                    fresh[m | bit][h] = jnp.where(clear, pltpu.roll(a, 128 - shift, 1), b)
            tiles = fresh
        for ny in range(16):
            local_ref[nx * RADIX + ny, :, :128] = tiles[ny][0]
            local_ref[nx * RADIX + ny, :, 128:] = tiles[ny][1]
        return carry

    lax.fori_loop(0, RADIX, regroup, 0)
    finish()


def lift(layout, coeffs, owner, count, column, potential):
    bands, _, sticks, _ = coeffs.shape
    index = jax.ShapeDtypeStruct(column.shape, jnp.int32)
    table, order = z_table(), y_order()
    n = layout.devices
    hbm = pl.BlockSpec(memory_space=pl.ANY)
    vmem = pl.BlockSpec(memory_space=pltpu.VMEM)
    return pl.pallas_call(
        functools.partial(lift_kernel, layout),
        out_shape=(
            jax.ShapeDtypeStruct((n, 2 * SLOTS, bands * sticks), jnp.float32),
            jax.ShapeDtypeStruct((COMBOS, SLOTS, PAD), jnp.float32),
            index, index, index,
        ),
        in_specs=[hbm, vmem, pl.BlockSpec(memory_space=pltpu.SMEM), vmem, hbm, hbm, hbm],
        out_specs=(hbm, vmem, vmem, vmem, vmem),
        scratch_shapes=[
            pltpu.VMEM((n, 2 * SLOTS, bands * sticks), jnp.float32),
            pltpu.VMEM((SLOTS, NX * NY), jnp.float32),
            pltpu.VMEM((NX * SLOTS, PAD), jnp.float32),
            pltpu.VMEM((NX * SLOTS, PAD), jnp.float32),
            pltpu.VMEM(coeffs.shape, jnp.float32),
            pltpu.VMEM(table.shape, jnp.bfloat16),
            pltpu.VMEM(order.shape, jnp.bfloat16),
            pltpu.SemaphoreType.DMA((n,)),
            pltpu.SemaphoreType.DMA((n,)),
            pltpu.SemaphoreType.DMA,
            pltpu.SemaphoreType.DMA((3,)),
        ],
        compiler_params=pltpu.CompilerParams(
            collective_id=0, has_side_effects=True, vmem_limit_bytes=60 * 2**20
        ),
    )(coeffs, owner, count, column, potential, jnp.asarray(table), jnp.asarray(order))


def back_kernel(
    layout, worked_ref, owner_ref, count_ref, table_hbm, out_ref, received, table_ref, send_sem, recv_sem, load_sem
):
    n, fft_size = layout.devices, layout.fft_size
    me = lax.axis_index("tg") * fft_size + lax.axis_index("fft")
    begin, finish = exchange(n, fft_size, me, worked_ref, received, send_sem, recv_sem)
    load = pltpu.make_async_copy(table_hbm, table_ref, load_sem)
    load.start()
    greet(n, fft_size, me)()
    begin()
    load.wait()
    per = PAD // SLOTS
    tables = [plane_tables(layout, owner_ref, table_ref, first * SLOTS) for first in range(0, n, per)]
    finish()

    bands, _, sticks, _ = out_ref.shape
    out_real = jnp.zeros((bands * sticks, PAD), jnp.float32)
    out_imag = jnp.zeros((bands * sticks, PAD), jnp.float32)

    def three(values, high, low):
        return dot(values[0], high) + dot(values[0], low) + dot(values[1], high)

    for index, first in enumerate(range(0, n, per)):
        high, low = tables[index]
        real = halves(received[first : first + per, :SLOTS].reshape(PAD, bands * sticks).T)
        imag = halves(received[first : first + per, SLOTS:].reshape(PAD, bands * sticks).T)
        cos_high, cos_low = high[:, :PAD], low[:, :PAD]
        sin_high, sin_low = high[:, PAD:], low[:, PAD:]
        out_real += three(real, cos_high, cos_low) + three(imag, sin_high, sin_low)
        out_imag += three(imag, cos_high, cos_low) - three(real, sin_high, sin_low)
    live = lax.broadcasted_iota(jnp.int32, (bands, sticks, NZ), 1) < count_ref[me]
    out_ref[:, 0] = jnp.where(live, out_real[:, :NZ].reshape(bands, sticks, NZ), 0.0)
    out_ref[:, 1] = jnp.where(live, out_imag[:, :NZ].reshape(bands, sticks, NZ), 0.0)


def lower(layout, worked, owner, count, shape):
    n = layout.devices
    table = z_table()
    hbm = pl.BlockSpec(memory_space=pl.ANY)
    vmem = pl.BlockSpec(memory_space=pltpu.VMEM)
    return pl.pallas_call(
        functools.partial(back_kernel, layout),
        out_shape=jax.ShapeDtypeStruct(shape, jnp.float32),
        in_specs=[hbm, vmem, pl.BlockSpec(memory_space=pltpu.SMEM), hbm],
        out_specs=vmem,
        scratch_shapes=[
            pltpu.VMEM(worked.shape, jnp.float32),
            pltpu.VMEM(table.shape, jnp.bfloat16),
            pltpu.SemaphoreType.DMA((n,)),
            pltpu.SemaphoreType.DMA((n,)),
            pltpu.SemaphoreType.DMA,
        ],
        compiler_params=pltpu.CompilerParams(
            collective_id=1, has_side_effects=True, vmem_limit_bytes=60 * 2**20
        ),
    )(worked, owner, count, jnp.asarray(table))


def per_device(coeffs, stick_count, stick_column, plane_owner, potential):
    layout = Layout(lax.axis_size("tg"), lax.axis_size("fft"), potential.shape[0])
    turned = jnp.swapaxes(coeffs, 2, 3)
    owner = plane_owner.reshape(1, NZ)
    column = stick_column.reshape(-1, 128)
    sticks, local, *places = lift(layout, turned, owner, stick_count, column, potential)
    places = [place.reshape(-1) for place in places]
    worked = on_grid(*places, stick_count, sticks, local)
    applied = lower(layout, worked, owner, stick_count, turned.shape)
    return jnp.swapaxes(applied, 2, 3)


def solution(mesh):
    in_specs = (P(None, None, None, ("tg", "fft")), P(), P(), P(), P("fft", None))
    out_specs = P(None, None, None, ("tg", "fft"))
    return jax.shard_map(
        per_device, mesh=mesh, in_specs=in_specs, out_specs=out_specs, check_vma=False
    )
```

```python
import functools
import math

import jax
import jax.numpy as jnp
import ml_dtypes
import numpy as np
from jax import lax
from jax.experimental import pallas as pl
from jax.experimental.pallas import tpu as pltpu
from jax.sharding import PartitionSpec as P

NX = 240
NY = 240
NZ = 240
PAD = 256
FOLD = 128
LANES = 64
RADIX = 16
ODD = 15
COMBOS = RADIX * RADIX
SLOTS = 8
GROUP = 8
UNROLL_Y = 2
BATCH = 4
MESH = pl.DeviceIdType.MESH


def split_table(table):
    table = table.astype(np.float32)
    high = table.astype(ml_dtypes.bfloat16)
    low = (table - high.astype(np.float32)).astype(ml_dtypes.bfloat16)
    return np.stack([high, low])


def z_table():
    indices = np.arange(NZ)
    angles = (indices[:, None] * indices[None, :] % NZ) * (2.0 * math.pi / NZ)
    table = np.zeros((PAD, 2 * PAD))
    table[:NZ, :NZ] = np.cos(angles) / math.sqrt(NZ)
    table[:NZ, PAD : PAD + NZ] = np.sin(angles) / math.sqrt(NZ)
    return split_table(table)


def folded_table():
    first = np.arange(ODD)
    table = np.zeros((PAD, PAD))
    for bx in range(ODD // 2 + 1):
        for by in range(ODD if bx else ODD // 2 + 1):
            i = ODD // 2 + 1 + (bx - 1) * ODD + by if bx else by
            angles = ((bx * first[:, None] + by * first[None, :]) % ODD) * (2.0 * math.pi / ODD)
            wide = np.zeros((2, RADIX, RADIX))
            wide[0, :ODD, :ODD] = np.cos(angles)
            wide[1, :ODD, :ODD] = -np.sin(angles)
            table[i] = wide[0].reshape(-1) / NX
            table[FOLD + i] = wide[1].reshape(-1) / NX
    return split_table(table)


def y_order():
    order = np.zeros((PAD, PAD), np.float32)
    y = np.arange(NY)
    order[y, (-y) % RADIX * RADIX + y % ODD] = 1.0
    return order.astype(ml_dtypes.bfloat16)


def halves(values):
    high = values.astype(jnp.bfloat16)
    low = (values - high.astype(jnp.float32)).astype(jnp.bfloat16)
    return high, low


def dot(a, b):
    return jnp.dot(a, b, preferred_element_type=jnp.float32)


def dot_last(a, b):
    return lax.dot_general(a, b, (((1,), (1,)), ((), ())), preferred_element_type=jnp.float32)


def butterfly(real, imag, sign):
    def four(xs):
        (ar, ai), (br, bi), (cr, ci), (dr, di) = xs
        er, ei, fr, fi = ar + cr, ai + ci, ar - cr, ai - ci
        gr, gi, hr, hi = br + dr, bi + di, br - dr, bi - di
        if sign > 0:
            return [(er + gr, ei + gi), (fr - hi, fi + hr), (er - gr, ei - gi), (fr + hi, fi - hr)]
        return [(er + gr, ei + gi), (fr + hi, fi - hr), (er - gr, ei - gi), (fr - hi, fi + hr)]

    def turn(x, power):
        r, i = x
        root = math.sqrt(0.5)
        if power == 0:
            return x
        if power == 4:
            return (-i, r) if sign > 0 else (i, -r)
        if power == 2:
            return ((r - i) * root, (r + i) * root) if sign > 0 else ((r + i) * root, (i - r) * root)
        if power == 6:
            return ((r + i) * -root, (r - i) * root) if sign > 0 else ((i - r) * root, (r + i) * -root)
        c = math.cos(2 * math.pi * power / 16)
        s = math.sin(2 * math.pi * power / 16) * sign
        return r * c - i * s, r * s + i * c

    inner = [four([(real[4 * n1 + n2], imag[4 * n1 + n2]) for n1 in range(4)]) for n2 in range(4)]
    out_real, out_imag = [None] * 16, [None] * 16
    for k1 in range(4):
        outer = four([turn(inner[n2][k1], n2 * k1) for n2 in range(4)])
        for k2 in range(4):
            out_real[k1 + 4 * k2], out_imag[k1 + 4 * k2] = outer[k2]
    return out_real, out_imag


def swap_halves(first, second):
    lower = lax.broadcasted_iota(jnp.int32, first.shape, first.ndim - 1) < 64
    first_turned = pltpu.roll(first, 64, first.ndim - 1)
    second_turned = pltpu.roll(second, 64, second.ndim - 1)
    return jnp.where(lower, first, second_turned), jnp.where(lower, first_turned, second)


def grid_kernel(
    source_ref, row_ref, half_ref, count_ref, sticks_hbm, local_hbm, table_hbm, turned_hbm, out_ref,
    columns, waves, ring, spare, staged, local_ref, table_ref, turned_ref, load_sem,
):
    loads = [
        pltpu.make_async_copy(source, target, load_sem.at[i])
        for i, (source, target) in enumerate(
            [(sticks_hbm, out_ref), (table_hbm, table_ref), (local_hbm, local_ref), (turned_hbm, turned_ref)]
        )
    ]
    for load in loads:
        load.start()
    devices = out_ref.shape[0]
    rows = devices * 32
    lane_half = lax.broadcasted_iota(jnp.int32, (1, 128), 1) // 64

    def clear(i, carry):
        columns[pl.ds(pl.multiple_of(i * PAD, PAD), PAD), :] = jnp.zeros((PAD, 128), jnp.float32)
        return carry

    lax.fori_loop(0, COMBOS // 2, clear, 0)
    loads[0].wait()

    def arrange(quad, carry):
        lines = [None] * 16
        for pair in range(2):
            d = quad * 4 + pair * 2
            for c in range(2):
                for t in range(2):
                    at = (pl.ds(c * 8, 8), pl.ds(t * 128, 128))
                    even, odd = swap_halves(out_ref[d, at[0], at[1]], out_ref[d + 1, at[0], at[1]])
                    lines[pair * 8 + c * 4 + t * 2] = even
                    lines[pair * 8 + c * 4 + t * 2 + 1] = odd
        block = jnp.concatenate(lines, axis=0).T
        base = pl.multiple_of(quad * 128, 128)
        staged[pl.ds(base, 128), :] = block
        staged[pl.ds(rows + base, 128), :] = pltpu.roll(block, 64, 1)
        return carry

    lax.fori_loop(0, devices // 4, arrange, 0, unroll=4)

    def over_live(work):
        def per_device(d, carry):
            def per_group(i, inner):
                for j in range(GROUP):
                    work(d * 64 + i * GROUP + j)
                return inner

            return lax.fori_loop(0, (count_ref[d] + GROUP - 1) // GROUP, per_group, carry)

        lax.fori_loop(0, devices, per_device, 0)

    def scatter(g):
        value = staged[pl.ds(source_ref[g], 1), :]
        pltpu.store(columns.at[pl.ds(row_ref[g], 1), :], value, mask=lane_half == half_ref[g])

    over_live(scatter)

    def folded(i, ax):
        base = pl.multiple_of((ax * (RADIX // 2) + i) * PAD, PAD)
        low_half = columns[pl.ds(base, FOLD), :].T
        high_half = columns[pl.ds(base + FOLD, FOLD), :].T
        odd = []
        for h in range(2):
            re, im = slice(h * 64, h * 64 + 32), slice(h * 64 + 32, h * 64 + 64)
            odd += [low_half[im] - high_half[im], high_half[re] - low_half[re]]
        return jnp.concatenate([low_half + high_half, jnp.concatenate(odd, axis=0)], axis=1)

    def three(values, table):
        high, low = halves(values)
        return dot(high, table[0]) + dot(high, table[1]) + dot(low, table[0])

    def forward(ring, i, first):
        total = three(jnp.concatenate([folded(i, first + k) for k in range(BATCH)], axis=0), table_ref)
        for l in range(2):
            at = pl.ds(pl.multiple_of((l * RADIX + first) * 128, 128), BATCH * 128)
            ring[at, :] = total[:, l * 128 : (l + 1) * 128]

    def in_ring(unit, k, c):
        h, b, l = unit // 8, unit // 2 % 4, unit % 2
        return pl.ds((l * RADIX + k) * 128 + h * 64 + c * 32 + b * 8, 8)

    def in_grid(i, unit, k, c):
        h, b, l = unit // 8, unit // 2 % 4, unit % 2
        base = pl.multiple_of(2 * i * LANES, 128)
        return pl.ds(base + (l * COMBOS + k * RADIX + h) * LANES + c * 32 + b * 8, 8)

    def forward_x(ring, i, unit):
        real = [ring[in_ring(unit, k, 0), :] for k in range(RADIX)]
        imag = [ring[in_ring(unit, k, 1), :] for k in range(RADIX)]
        real, imag = butterfly(real, imag, 1)
        for k in range(RADIX):
            waves[in_grid(i, unit, k, 0), :] = real[k]
            waves[in_grid(i, unit, k, 1), :] = imag[k]

    def backward_x(ring, i, unit):
        real = [columns[in_grid(i, unit, k, 0), :] for k in range(RADIX)]
        imag = [columns[in_grid(i, unit, k, 1), :] for k in range(RADIX)]
        real, imag = butterfly(real, imag, -1)
        for k in range(RADIX):
            ring[in_ring(unit, k, 0), :] = real[k]
            ring[in_ring(unit, k, 1), :] = imag[k]

    def backward(ring, i, start):
        values = jnp.concatenate(
            [ring[pl.ds(pl.multiple_of((l * RADIX + start) * 128, 128), BATCH * 128), :] for l in range(2)], axis=1
        )
        total = three(values, turned_ref)
        for k in range(BATCH):
            cosine, sine = total[k * 128 : (k + 1) * 128, :FOLD], total[k * 128 : (k + 1) * 128, FOLD:]
            first, second = [], []
            for h in range(2):
                re, im = slice(h * 64, h * 64 + 32), slice(h * 64 + 32, h * 64 + 64)
                first += [cosine[re] - sine[im], cosine[im] + sine[re]]
                second += [cosine[re] + sine[im], cosine[im] - sine[re]]
            base = pl.multiple_of(((start + k) * (RADIX // 2) + i) * PAD, PAD)
            waves[pl.ds(base, FOLD), :] = jnp.concatenate(first, axis=0).T
            waves[pl.ds(base + FOLD, FOLD), :] = jnp.concatenate(second, axis=0).T

    slabs = RADIX // 2

    def first_slab(j, carry):
        forward(ring, 0, j * BATCH)
        return carry

    def forward_step(i, here, there):
        for j in range(RADIX):
            if j % BATCH == 0:
                forward(there, i + 1, j)
            forward_x(here, i, j)

    def forward_slabs(t, carry):
        forward_step(2 * t, ring, spare)
        forward_step(2 * t + 1, spare, ring)
        return carry

    loads[1].wait()
    lax.fori_loop(0, RADIX // BATCH, first_slab, 0, unroll=RADIX // BATCH)
    lax.fori_loop(0, slabs // 2 - 1, forward_slabs, 0)
    forward_step(slabs - 2, ring, spare)
    for j in range(RADIX):
        forward_x(spare, slabs - 1, j)

    def along_y(ax, carry):
        for l in range(2):
            lanes = pl.ds(l * 128, 128)
            for b in range(4):
                def at(k, c):
                    base = pl.multiple_of((l * COMBOS + ax * RADIX) * LANES, LANES)
                    return pl.ds(base + k * LANES + c * 32 + b * 8, 8)

                real = [waves[at(k, 0), :] for k in range(RADIX)]
                imag = [waves[at(k, 1), :] for k in range(RADIX)]
                real, imag = butterfly(real, imag, 1)
                local = [local_ref[ax * RADIX + k, :, lanes] for k in range(RADIX)]
                real = [value * local[k] for k, value in enumerate(real)]
                imag = [value * local[k] for k, value in enumerate(imag)]
                real, imag = butterfly(real, imag, -1)
                for k in range(RADIX):
                    columns[at(k, 0), :] = real[k]
                    columns[at(k, 1), :] = imag[k]
        return carry

    loads[2].wait()
    loads[3].wait()
    lax.fori_loop(0, RADIX, along_y, 0, unroll=UNROLL_Y)

    for j in range(RADIX):
        backward_x(ring, 0, j)

    def backward_step(i, here, there):
        for j in range(RADIX):
            if j % BATCH == 0:
                backward(here, i, j)
            backward_x(there, jnp.minimum(i + 1, slabs - 1), j)

    def backward_slabs(t, carry):
        backward_step(2 * t, ring, spare)
        backward_step(2 * t + 1, spare, ring)
        return carry

    lax.fori_loop(0, slabs // 2, backward_slabs, 0)
    staged[...] = jnp.zeros_like(staged)

    def gather(g):
        value = waves[pl.ds(row_ref[g], 1), :]
        pltpu.store(staged.at[pl.ds(source_ref[g], 1), :], value, mask=lane_half == half_ref[g])

    over_live(gather)

    def restore(quad, carry):
        base = pl.multiple_of(quad * 128, 128)
        block = staged[pl.ds(base, 128), :] + pltpu.roll(staged[pl.ds(rows + base, 128), :], 64, 1)
        block = block.T
        for pair in range(2):
            d = quad * 4 + pair * 2
            for c in range(2):
                for t in range(2):
                    line = (pair * 8 + c * 4 + t * 2) * 8
                    first, second = swap_halves(block[line : line + 8], block[line + 8 : line + 16])
                    at = (pl.ds(c * 8, 8), pl.ds(t * 128, 128))
                    out_ref[d, at[0], at[1]] = first
                    out_ref[d + 1, at[0], at[1]] = second
        return carry

    lax.fori_loop(0, devices // 4, restore, 0, unroll=4)


def on_grid(source, row, half, count, sticks, local):
    table = folded_table()
    turned = np.swapaxes(table, 1, 2)
    rows = sticks.shape[0] * 32
    smem = pl.BlockSpec(memory_space=pltpu.SMEM)
    vmem = pl.BlockSpec(memory_space=pltpu.VMEM)
    return pl.pallas_call(
        grid_kernel,
        out_shape=jax.ShapeDtypeStruct(sticks.shape, jnp.float32),
        in_specs=[smem] * 4 + [pl.BlockSpec(memory_space=pl.ANY)] * 4,
        out_specs=vmem,
        scratch_shapes=[
            pltpu.VMEM((COMBOS // 2 * PAD, 128), jnp.float32),
            pltpu.VMEM((COMBOS // 2 * PAD, 128), jnp.float32),
            pltpu.VMEM((2 * RADIX * 128, 128), jnp.float32),
            pltpu.VMEM((2 * RADIX * 128, 128), jnp.float32),
            pltpu.VMEM((2 * rows, 128), jnp.float32),
            pltpu.VMEM(local.shape, jnp.float32),
            pltpu.VMEM(table.shape, jnp.bfloat16),
            pltpu.VMEM(table.shape, jnp.bfloat16),
            pltpu.SemaphoreType.DMA((4,)),
        ],
        compiler_params=pltpu.CompilerParams(vmem_limit_bytes=60 * 2**20),
    )(source, row, half, count, sticks, local, jnp.asarray(table), jnp.asarray(turned))


class Layout:
    def __init__(self, tg_size, fft_size, plane_slots):
        self.tg_size, self.fft_size, self.plane_slots = tg_size, fft_size, plane_slots
        self.devices = tg_size * fft_size
        self.chunk = -(-plane_slots // tg_size)
        self.starts = [t * self.chunk // SLOTS * SLOTS for t in range(tg_size)]


def greet(n, fft_size, me):
    barrier = pltpu.get_barrier_semaphore()

    def signal(i, carry):
        other = lax.rem(me + i, n)
        pl.semaphore_signal(
            barrier, inc=1, device_id=(other // fft_size, lax.rem(other, fft_size)), device_id_type=MESH
        )
        return carry

    lax.fori_loop(1, n, signal, 0)
    return lambda: pl.semaphore_wait(barrier, n - 1)


def exchange(n, fft_size, me, source, target, send_sem, recv_sem):
    def copy(i):
        other = lax.rem(me + i, n)
        return pltpu.make_async_remote_copy(
            src_ref=source.at[other], dst_ref=target.at[me], send_sem=send_sem.at[i], recv_sem=recv_sem.at[i],
            device_id=(other // fft_size, lax.rem(other, fft_size)), device_id_type=MESH,
        )

    def start(i, carry):
        copy(i).start()
        return carry

    def wait(i, carry):
        copy(i).wait()
        return carry

    own = pltpu.make_async_copy(source.at[me], target.at[me], send_sem.at[0])

    def begin():
        lax.fori_loop(1, n, start, 0)
        own.start()

    def finish():
        own.wait()
        lax.fori_loop(1, n, wait, 0)

    return begin, finish


def plane_row(layout, owner_ref):
    outside = jnp.full((1, PAD - NZ), 2 * layout.fft_size, jnp.int32)
    owner = jnp.concatenate([owner_ref[...], outside], axis=1).astype(jnp.float32)
    owner = jnp.broadcast_to(owner, (PAD, PAD))
    index = lax.broadcasted_iota(jnp.int32, (PAD, PAD), 0)
    same = (owner == owner.T) & (index < lax.broadcasted_iota(jnp.int32, (PAD, PAD), 1))
    rank = jnp.sum(jnp.where(same, 1.0, 0.0), axis=0, keepdims=True)
    group = jnp.zeros_like(rank)
    offset = jnp.zeros_like(rank)
    for t in range(1, layout.tg_size):
        beyond = rank >= float(t * layout.chunk)
        group = jnp.where(beyond, float(t), group)
        offset = jnp.where(beyond, float(layout.starts[t]), offset)
    return (group * layout.fft_size + owner[:1]) * SLOTS + rank - offset


def plane_pick(row, first):
    index = lax.broadcasted_iota(jnp.int32, (PAD, PAD), 0)
    return jnp.where(index.astype(jnp.float32) + float(first) == row, 1.0, 0.0).astype(jnp.bfloat16)


def plane_tables(pick, table_ref):
    return dot(pick, table_ref[0]).astype(jnp.bfloat16), dot(pick, table_ref[1]).astype(jnp.bfloat16)


def divided(value, divisor):
    quotient = jnp.floor((value + 0.5) * (1.0 / divisor))
    return quotient, value - quotient * divisor


def stick_places(count_ref, column_ref, source_ref, row_ref, half_ref):
    rows = column_ref.shape[0]
    lane = lax.broadcasted_iota(jnp.int32, (8, 128), 1)
    sublane = lax.broadcasted_iota(jnp.int32, (8, 128), 0)
    within = lane % 64
    middle, last = float(ODD // 2), float(FOLD - 1)

    def step(i, carry):
        at = pl.ds(pl.multiple_of(i * 8, 8), 8)
        count = jnp.zeros((8, 128), jnp.int32)
        for r in range(8):
            for h in range(2):
                count = jnp.where((sublane == r) & (lane // 64 == h), count_ref[i * 16 + 2 * r + h], count)
        x, y = divided(column_ref[at, :].astype(jnp.float32), float(NY))
        ax, ay = divided(x, float(RADIX))[1], divided(y, float(RADIX))[1]
        bx, by = divided(x, float(ODD))[1], divided(y, float(ODD))[1]
        negative = (bx > middle) | ((bx == 0.0) & (by > middle))
        bx = jnp.where(negative & (bx > 0.0), ODD - bx, bx)
        by = jnp.where(negative & (by > 0.0), ODD - by, by)
        place = jnp.where(bx == 0.0, by, middle + 1.0 + (bx - 1.0) * ODD + by)
        place = place + jnp.where(negative, float(FOLD), 0.0)
        pair, half = divided(ax * RADIX + ay, 2.0)
        row_ref[at, :] = jnp.where(within < count, pair * PAD + place, last).astype(jnp.int32)
        half = half.astype(jnp.int32)
        half_ref[at, :] = half
        slot_row = i * 8 + sublane
        source = slot_row // 2 * 128 + lane
        source_ref[at, :] = source + jnp.where(slot_row % 2 != half, rows * 64, 0)
        return carry

    lax.fori_loop(0, rows // 8, step, 0)


def lift_kernel(
    layout, coeffs_hbm, owner_ref, count_ref, column_ref, potential_ref, table_hbm, order_hbm,
    out_ref, local_out, source_ref, row_ref, half_ref,
    parts, local_ref, slab, lines, spread, coeffs_ref, table_ref, order_ref, send_sem, recv_sem, slab_sem, load_sem, store_sem,
):
    n, fft_size = layout.devices, layout.fft_size
    tg = lax.axis_index("tg")
    me = tg * fft_size + lax.axis_index("fft")
    loads = [
        pltpu.make_async_copy(source, target, load_sem.at[i])
        for i, (source, target) in enumerate(
            [(coeffs_hbm, coeffs_ref), (table_hbm, table_ref), (order_hbm, order_ref)]
        )
    ]
    for load in loads:
        load.start()
    greeted = greet(n, fft_size, me)

    slabs = []
    for t in range(layout.tg_size):
        start = layout.starts[t]
        count = min(SLOTS, layout.plane_slots - start)
        slabs.append((t, count, pltpu.make_async_copy(
            potential_ref.at[pl.ds(start, count), :], slab.at[pl.ds(0, count), :], slab_sem
        )))
    for t, count, copy in slabs:
        @pl.when(tg == t)
        def _():
            if count < SLOTS:
                slab[...] = jnp.zeros_like(slab)
            copy.start()

    per = PAD // SLOTS
    row = plane_row(layout, owner_ref)
    picks = [plane_pick(row, first * SLOTS) for first in range(0, n, per)]
    loads[1].wait()
    tables = [plane_tables(pick, table_ref) for pick in picks]
    loads[0].wait()
    bands, _, sticks, _ = coeffs_ref.shape
    real = halves(coeffs_ref[:, 0].reshape(bands * sticks, NZ))
    imag = halves(coeffs_ref[:, 1].reshape(bands * sticks, NZ))

    def three(high, low, values):
        return dot_last(high, values[0]) + dot_last(low, values[0]) + dot_last(high, values[1])

    for first in range(0, n, per):
        high, low = tables[first // per]
        cos_high, cos_low = high[:, :NZ], low[:, :NZ]
        sin_high, sin_low = high[:, PAD : PAD + NZ], low[:, PAD : PAD + NZ]
        up_real = three(cos_high, cos_low, real) - three(sin_high, sin_low, imag)
        up_imag = three(sin_high, sin_low, real) + three(cos_high, cos_low, imag)
        parts[first : first + per, :SLOTS] = up_real.reshape(per, SLOTS, bands * sticks)
        parts[first : first + per, SLOTS:] = up_imag.reshape(per, SLOTS, bands * sticks)

    begin, finish = exchange(n, fft_size, me, parts, out_ref, send_sem, recv_sem)
    greeted()
    begin()

    stick_places(count_ref, column_ref, source_ref, row_ref, half_ref)
    loads[2].wait()
    for t, count, copy in slabs:
        @pl.when(tg == t)
        def _():
            copy.wait()

    lines[:, NY:] = jnp.zeros((NX * SLOTS, PAD - NY), jnp.float32)

    def cut(q, carry):
        wide = slab[:, pl.ds(pl.multiple_of(q * 8 * NY, 128), 8 * NY)]
        for r in range(8):
            lines[pl.ds(pl.multiple_of(q * 8 * SLOTS, 8 * SLOTS) + r * SLOTS, SLOTS), :NY] = wide[:, r * NY : (r + 1) * NY]
        return carry

    lax.fori_loop(0, NX // 8, cut, 0)
    order = order_ref[...]

    def reorder(i, carry):
        at = pl.ds(pl.multiple_of(i * 128, 128), 128)
        values = lines[at, :]
        high, low = halves(values)
        rest = (values - high.astype(jnp.float32) - low.astype(jnp.float32)).astype(jnp.bfloat16)
        spread[at, :] = dot(high, order) + dot(low, order) + dot(rest, order)
        return carry

    lax.fori_loop(0, NX * SLOTS // 128, reorder, 0)
    lane_block = lax.broadcasted_iota(jnp.int32, (SLOTS, 128), 1) // RADIX

    def regroup(nx, carry):
        tiles = []
        for mx in range(ODD):
            x = lax.rem(nx * ODD + mx * RADIX, NX)
            at = pl.ds(pl.multiple_of(x * SLOTS, SLOTS), SLOTS)
            tiles.append([spread[at, :128], spread[at, 128:]])
        tiles.append([jnp.zeros((SLOTS, 128), jnp.float32)] * 2)
        tiles = [[tiles[m % 8 + 8 * (h % 2)][m // 8] for h in range(2)] for m in range(16)]
        for bit in (4, 2, 1):
            shift = bit * RADIX
            clear = lane_block % (2 * bit) < bit
            fresh = [[None, None] for _ in range(16)]
            for m in range(16):
                if m & bit:
                    continue
                for h in range(2):
                    a, b = tiles[m][h], tiles[m | bit][h]
                    fresh[m][h] = jnp.where(clear, a, pltpu.roll(b, shift, 1))
                    fresh[m | bit][h] = jnp.where(clear, pltpu.roll(a, 128 - shift, 1), b)
            tiles = fresh
        for ny in range(16):
            local_ref[nx * RADIX + ny, :, :128] = tiles[ny][0]
            local_ref[nx * RADIX + ny, :, 128:] = tiles[ny][1]
        return carry

    lax.fori_loop(0, RADIX, regroup, 0)
    store = pltpu.make_async_copy(local_ref, local_out, store_sem)
    store.start()
    store.wait()
    finish()


def lift(layout, coeffs, owner, count, column, potential):
    bands, _, sticks, _ = coeffs.shape
    index = jax.ShapeDtypeStruct(column.shape, jnp.int32)
    table, order = z_table(), y_order()
    n = layout.devices
    hbm = pl.BlockSpec(memory_space=pl.ANY)
    vmem = pl.BlockSpec(memory_space=pltpu.VMEM)
    return pl.pallas_call(
        functools.partial(lift_kernel, layout),
        out_shape=(
            jax.ShapeDtypeStruct((n, 2 * SLOTS, bands * sticks), jnp.float32),
            jax.ShapeDtypeStruct((COMBOS, SLOTS, PAD), jnp.float32),
            index, index, index,
        ),
        in_specs=[hbm, vmem, pl.BlockSpec(memory_space=pltpu.SMEM), vmem, hbm, hbm, hbm],
        out_specs=(hbm, hbm, vmem, vmem, vmem),
        scratch_shapes=[
            pltpu.VMEM((n, 2 * SLOTS, bands * sticks), jnp.float32),
            pltpu.VMEM((COMBOS, SLOTS, PAD), jnp.float32),
            pltpu.VMEM((SLOTS, NX * NY), jnp.float32),
            pltpu.VMEM((NX * SLOTS, PAD), jnp.float32),
            pltpu.VMEM((NX * SLOTS, PAD), jnp.float32),
            pltpu.VMEM(coeffs.shape, jnp.float32),
            pltpu.VMEM(table.shape, jnp.bfloat16),
            pltpu.VMEM(order.shape, jnp.bfloat16),
            pltpu.SemaphoreType.DMA((n,)),
            pltpu.SemaphoreType.DMA((n,)),
            pltpu.SemaphoreType.DMA,
            pltpu.SemaphoreType.DMA((3,)),
            pltpu.SemaphoreType.DMA,
        ],
        compiler_params=pltpu.CompilerParams(
            collective_id=0, has_side_effects=True, vmem_limit_bytes=60 * 2**20
        ),
    )(coeffs, owner, count, column, potential, jnp.asarray(table), jnp.asarray(order))


def back_kernel(
    layout, worked_ref, owner_ref, count_ref, table_hbm, out_ref, received, table_ref, send_sem, recv_sem, load_sem
):
    n, fft_size = layout.devices, layout.fft_size
    me = lax.axis_index("tg") * fft_size + lax.axis_index("fft")
    begin, finish = exchange(n, fft_size, me, worked_ref, received, send_sem, recv_sem)
    load = pltpu.make_async_copy(table_hbm, table_ref, load_sem)
    load.start()
    greet(n, fft_size, me)()
    begin()
    load.wait()
    per = PAD // SLOTS
    row = plane_row(layout, owner_ref)
    tables = [plane_tables(plane_pick(row, first * SLOTS), table_ref) for first in range(0, n, per)]
    finish()

    bands, _, sticks, _ = out_ref.shape
    out_real = jnp.zeros((bands * sticks, PAD), jnp.float32)
    out_imag = jnp.zeros((bands * sticks, PAD), jnp.float32)

    def three(values, high, low):
        return dot(values[0], high) + dot(values[0], low) + dot(values[1], high)

    for index, first in enumerate(range(0, n, per)):
        high, low = tables[index]
        real = halves(received[first : first + per, :SLOTS].reshape(PAD, bands * sticks).T)
        imag = halves(received[first : first + per, SLOTS:].reshape(PAD, bands * sticks).T)
        cos_high, cos_low = high[:, :PAD], low[:, :PAD]
        sin_high, sin_low = high[:, PAD:], low[:, PAD:]
        out_real += three(real, cos_high, cos_low) + three(imag, sin_high, sin_low)
        out_imag += three(imag, cos_high, cos_low) - three(real, sin_high, sin_low)
    live = lax.broadcasted_iota(jnp.int32, (bands, sticks, NZ), 1) < count_ref[me]
    out_ref[:, 0] = jnp.where(live, out_real[:, :NZ].reshape(bands, sticks, NZ), 0.0)
    out_ref[:, 1] = jnp.where(live, out_imag[:, :NZ].reshape(bands, sticks, NZ), 0.0)


def lower(layout, worked, owner, count, shape):
    n = layout.devices
    table = z_table()
    hbm = pl.BlockSpec(memory_space=pltpu.HBM)
    vmem = pl.BlockSpec(memory_space=pltpu.VMEM)
    return pl.pallas_call(
        functools.partial(back_kernel, layout),
        out_shape=jax.ShapeDtypeStruct(shape, jnp.float32),
        in_specs=[hbm, vmem, pl.BlockSpec(memory_space=pltpu.SMEM), hbm],
        out_specs=vmem,
        scratch_shapes=[
            pltpu.VMEM(worked.shape, jnp.float32),
            pltpu.VMEM(table.shape, jnp.bfloat16),
            pltpu.SemaphoreType.DMA((n,)),
            pltpu.SemaphoreType.DMA((n,)),
            pltpu.SemaphoreType.DMA,
        ],
        compiler_params=pltpu.CompilerParams(
            collective_id=1, has_side_effects=True, vmem_limit_bytes=40 * 2**20
        ),
    )(worked, owner, count, jnp.asarray(table))


def per_device(coeffs, stick_count, stick_column, plane_owner, potential):
    layout = Layout(lax.axis_size("tg"), lax.axis_size("fft"), potential.shape[0])
    turned = jnp.swapaxes(coeffs, 2, 3)
    owner = plane_owner.reshape(1, NZ)
    column = stick_column.reshape(-1, 128)
    sticks, local, *places = lift(layout, turned, owner, stick_count, column, potential)
    places = [place.reshape(-1) for place in places]
    worked = on_grid(*places, stick_count, sticks, local)
    applied = lower(layout, worked, owner, stick_count, turned.shape)
    return jnp.swapaxes(applied, 2, 3)


def solution(mesh):
    in_specs = (P(None, None, None, ("tg", "fft")), P(), P(), P(), P("fft", None))
    out_specs = P(None, None, None, ("tg", "fft"))
    return jax.shard_map(
        per_device, mesh=mesh, in_specs=in_specs, out_specs=out_specs, check_vma=False
    )
```

```python
import functools
import math

import jax
import jax.numpy as jnp
import ml_dtypes
import numpy as np
from jax import lax
from jax.experimental import pallas as pl
from jax.experimental.pallas import tpu as pltpu
from jax.sharding import PartitionSpec as P

NX = 240
NY = 240
NZ = 240
PAD = 256
FOLD = 128
LANES = 64
RADIX = 16
ODD = 15
COMBOS = RADIX * RADIX
SLOTS = 8
GROUP = 8
UNROLL_Y = 2
BATCH = 4
MESH = pl.DeviceIdType.MESH


def split_table(table):
    table = table.astype(np.float32)
    high = table.astype(ml_dtypes.bfloat16)
    low = (table - high.astype(np.float32)).astype(ml_dtypes.bfloat16)
    return np.stack([high, low])


def z_table():
    indices = np.arange(NZ)
    angles = (indices[:, None] * indices[None, :] % NZ) * (2.0 * math.pi / NZ)
    table = np.zeros((PAD, 2 * PAD))
    table[:NZ, :NZ] = np.cos(angles) / math.sqrt(NZ)
    table[:NZ, PAD : PAD + NZ] = np.sin(angles) / math.sqrt(NZ)
    return split_table(table)


def folded_table():
    first = np.arange(ODD)
    table = np.zeros((PAD, PAD))
    for bx in range(ODD // 2 + 1):
        for by in range(ODD if bx else ODD // 2 + 1):
            i = ODD // 2 + 1 + (bx - 1) * ODD + by if bx else by
            angles = ((bx * first[:, None] + by * first[None, :]) % ODD) * (2.0 * math.pi / ODD)
            wide = np.zeros((2, RADIX, RADIX))
            wide[0, :ODD, :ODD] = np.cos(angles)
            wide[1, :ODD, :ODD] = -np.sin(angles)
            table[i] = wide[0].reshape(-1) / NX
            table[FOLD + i] = wide[1].reshape(-1) / NX
    return split_table(table)


def y_order():
    order = np.zeros((PAD, PAD), np.float32)
    y = np.arange(NY)
    order[y, (-y) % RADIX * RADIX + y % ODD] = 1.0
    return order.astype(ml_dtypes.bfloat16)


def halves(values):
    high = values.astype(jnp.bfloat16)
    low = (values - high.astype(jnp.float32)).astype(jnp.bfloat16)
    return high, low


def dot(a, b):
    return jnp.dot(a, b, preferred_element_type=jnp.float32)


def dot_last(a, b):
    return lax.dot_general(a, b, (((1,), (1,)), ((), ())), preferred_element_type=jnp.float32)


def butterfly(real, imag, sign):
    def four(xs):
        (ar, ai), (br, bi), (cr, ci), (dr, di) = xs
        er, ei, fr, fi = ar + cr, ai + ci, ar - cr, ai - ci
        gr, gi, hr, hi = br + dr, bi + di, br - dr, bi - di
        if sign > 0:
            return [(er + gr, ei + gi), (fr - hi, fi + hr), (er - gr, ei - gi), (fr + hi, fi - hr)]
        return [(er + gr, ei + gi), (fr + hi, fi - hr), (er - gr, ei - gi), (fr - hi, fi + hr)]

    def turn(x, power):
        r, i = x
        root = math.sqrt(0.5)
        if power == 0:
            return x
        if power == 4:
            return (-i, r) if sign > 0 else (i, -r)
        if power == 2:
            return ((r - i) * root, (r + i) * root) if sign > 0 else ((r + i) * root, (i - r) * root)
        if power == 6:
            return ((r + i) * -root, (r - i) * root) if sign > 0 else ((i - r) * root, (r + i) * -root)
        c = math.cos(2 * math.pi * power / 16)
        s = math.sin(2 * math.pi * power / 16) * sign
        return r * c - i * s, r * s + i * c

    inner = [four([(real[4 * n1 + n2], imag[4 * n1 + n2]) for n1 in range(4)]) for n2 in range(4)]
    out_real, out_imag = [None] * 16, [None] * 16
    for k1 in range(4):
        outer = four([turn(inner[n2][k1], n2 * k1) for n2 in range(4)])
        for k2 in range(4):
            out_real[k1 + 4 * k2], out_imag[k1 + 4 * k2] = outer[k2]
    return out_real, out_imag


def swap_halves(first, second):
    lower = lax.broadcasted_iota(jnp.int32, first.shape, first.ndim - 1) < 64
    first_turned = pltpu.roll(first, 64, first.ndim - 1)
    second_turned = pltpu.roll(second, 64, second.ndim - 1)
    return jnp.where(lower, first, second_turned), jnp.where(lower, first_turned, second)


def grid_kernel(
    source_ref, row_ref, half_ref, count_ref, sticks_hbm, local_hbm, table_hbm, turned_hbm, out_ref,
    columns, waves, ring, spare, prep_even, prep_odd, total_even, total_odd, staged, local_ref, table_ref, turned_ref, load_sem,
):
    loads = [
        pltpu.make_async_copy(source, target, load_sem.at[i])
        for i, (source, target) in enumerate(
            [(sticks_hbm, out_ref), (table_hbm, table_ref), (local_hbm, local_ref), (turned_hbm, turned_ref)]
        )
    ]
    for load in loads:
        load.start()
    devices = out_ref.shape[0]
    rows = devices * 32
    lane_half = lax.broadcasted_iota(jnp.int32, (1, 128), 1) // 64

    def clear(i, carry):
        columns[pl.ds(pl.multiple_of(i * PAD, PAD), PAD), :] = jnp.zeros((PAD, 128), jnp.float32)
        return carry

    lax.fori_loop(0, COMBOS // 2, clear, 0)
    loads[0].wait()

    def arrange(quad, carry):
        lines = [None] * 16
        for pair in range(2):
            d = quad * 4 + pair * 2
            for c in range(2):
                for t in range(2):
                    at = (pl.ds(c * 8, 8), pl.ds(t * 128, 128))
                    even, odd = swap_halves(out_ref[d, at[0], at[1]], out_ref[d + 1, at[0], at[1]])
                    lines[pair * 8 + c * 4 + t * 2] = even
                    lines[pair * 8 + c * 4 + t * 2 + 1] = odd
        block = jnp.concatenate(lines, axis=0).T
        base = pl.multiple_of(quad * 128, 128)
        staged[pl.ds(base, 128), :] = block
        staged[pl.ds(rows + base, 128), :] = pltpu.roll(block, 64, 1)
        return carry

    lax.fori_loop(0, devices // 4, arrange, 0, unroll=4)

    def over_live(work):
        def per_device(d, carry):
            def per_group(i, inner):
                for j in range(GROUP):
                    work(d * 64 + i * GROUP + j)
                return inner

            return lax.fori_loop(0, (count_ref[d] + GROUP - 1) // GROUP, per_group, carry)

        lax.fori_loop(0, devices, per_device, 0)

    def scatter(g):
        value = staged[pl.ds(source_ref[g], 1), :]
        pltpu.store(columns.at[pl.ds(row_ref[g], 1), :], value, mask=lane_half == half_ref[g])

    over_live(scatter)

    def folded(i, ax):
        base = pl.multiple_of((ax * (RADIX // 2) + i) * PAD, PAD)
        low_half = columns[pl.ds(base, FOLD), :].T
        high_half = columns[pl.ds(base + FOLD, FOLD), :].T
        odd = []
        for h in range(2):
            re, im = slice(h * 64, h * 64 + 32), slice(h * 64 + 32, h * 64 + 64)
            odd += [low_half[im] - high_half[im], high_half[re] - low_half[re]]
        return jnp.concatenate([low_half + high_half, jnp.concatenate(odd, axis=0)], axis=1)

    def three(high, low, table):
        return dot(high, table[0]) + dot(high, table[1]) + dot(low, table[0])

    def prepare(i, first, prep):
        for k in range(BATCH):
            high, low = halves(folded(i, first + k))
            prep[0, k * 128 : (k + 1) * 128, :] = high
            prep[1, k * 128 : (k + 1) * 128, :] = low

    def forward(ring, first, prep):
        total = three(prep[0], prep[1], table_ref)
        for l in range(2):
            at = pl.ds((l * RADIX + first) * 128, BATCH * 128)
            ring[at, :] = total[:, l * 128 : (l + 1) * 128]

    def in_ring(unit, k, c):
        h, b, l = unit // 8, unit // 2 % 4, unit % 2
        return pl.ds((l * RADIX + k) * 128 + h * 64 + c * 32 + b * 8, 8)

    def in_grid(i, unit, k, c):
        h, b, l = unit // 8, unit // 2 % 4, unit % 2
        base = pl.multiple_of(2 * i * LANES, 128)
        return pl.ds(base + (l * COMBOS + k * RADIX + h) * LANES + c * 32 + b * 8, 8)

    def forward_x(ring, i, unit):
        real = [ring[in_ring(unit, k, 0), :] for k in range(RADIX)]
        imag = [ring[in_ring(unit, k, 1), :] for k in range(RADIX)]
        real, imag = butterfly(real, imag, 1)
        for k in range(RADIX):
            waves[in_grid(i, unit, k, 0), :] = real[k]
            waves[in_grid(i, unit, k, 1), :] = imag[k]

    def backward_x(ring, i, unit):
        real = [columns[in_grid(i, unit, k, 0), :] for k in range(RADIX)]
        imag = [columns[in_grid(i, unit, k, 1), :] for k in range(RADIX)]
        real, imag = butterfly(real, imag, -1)
        for k in range(RADIX):
            ring[in_ring(unit, k, 0), :] = real[k]
            ring[in_ring(unit, k, 1), :] = imag[k]

    def backward(ring, start, total):
        values = jnp.concatenate(
            [ring[pl.ds((l * RADIX + start) * 128, BATCH * 128), :] for l in range(2)], axis=1
        )
        total[...] = three(*halves(values), turned_ref)

    def unfold(i, start, total):
        for k in range(BATCH):
            cosine, sine = total[k * 128 : (k + 1) * 128, :FOLD], total[k * 128 : (k + 1) * 128, FOLD:]
            first, second = [], []
            for h in range(2):
                re, im = slice(h * 64, h * 64 + 32), slice(h * 64 + 32, h * 64 + 64)
                first += [cosine[re] - sine[im], cosine[im] + sine[re]]
                second += [cosine[re] + sine[im], cosine[im] - sine[re]]
            base = pl.multiple_of(((start + k) * (RADIX // 2) + i) * PAD, PAD)
            waves[pl.ds(base, FOLD), :] = jnp.concatenate(first, axis=0).T
            waves[pl.ds(base + FOLD, FOLD), :] = jnp.concatenate(second, axis=0).T

    slabs = RADIX // 2

    preps, totals = (prep_even, prep_odd), (total_even, total_odd)
    groups = RADIX // BATCH

    def forward_group(i, q, target):
        prepare(jnp.minimum(i + (q + 1) // groups, slabs - 1), (q + 1) % groups * BATCH, preps[(q + 1) % 2])
        forward(target, q * BATCH, preps[q % 2])

    def forward_step(i, here, there):
        for j in range(RADIX):
            if j % BATCH == 0:
                forward_group(i + 1, j // BATCH, there)
            forward_x(here, i, j)

    def forward_slabs(t, carry):
        forward_step(2 * t, ring, spare)
        forward_step(2 * t + 1, spare, ring)
        return carry

    loads[1].wait()
    prepare(0, 0, prep_even)
    for q in range(groups):
        forward_group(0, q, ring)
    lax.fori_loop(0, slabs // 2 - 1, forward_slabs, 0)
    forward_step(slabs - 2, ring, spare)
    for j in range(RADIX):
        forward_x(spare, slabs - 1, j)

    def along_y(ax, carry):
        for l in range(2):
            lanes = pl.ds(l * 128, 128)
            for b in range(4):
                def at(k, c):
                    base = pl.multiple_of((l * COMBOS + ax * RADIX) * LANES, LANES)
                    return pl.ds(base + k * LANES + c * 32 + b * 8, 8)

                real = [waves[at(k, 0), :] for k in range(RADIX)]
                imag = [waves[at(k, 1), :] for k in range(RADIX)]
                real, imag = butterfly(real, imag, 1)
                local = [local_ref[ax * RADIX + k, :, lanes] for k in range(RADIX)]
                real = [value * local[k] for k, value in enumerate(real)]
                imag = [value * local[k] for k, value in enumerate(imag)]
                real, imag = butterfly(real, imag, -1)
                for k in range(RADIX):
                    columns[at(k, 0), :] = real[k]
                    columns[at(k, 1), :] = imag[k]
        return carry

    loads[2].wait()
    loads[3].wait()
    lax.fori_loop(0, RADIX, along_y, 0, unroll=UNROLL_Y)

    for j in range(RADIX):
        backward_x(ring, 0, j)

    def backward_step(i, here, there):
        for j in range(RADIX):
            if j % BATCH == 0:
                q = j // BATCH
                unfold(i if q else jnp.maximum(i - 1, 0), (q - 1) % groups * BATCH, totals[(q - 1) % 2])
                backward(here, j, totals[q % 2])
            backward_x(there, jnp.minimum(i + 1, slabs - 1), j)

    def backward_slabs(t, carry):
        backward_step(2 * t, ring, spare)
        backward_step(2 * t + 1, spare, ring)
        return carry

    lax.fori_loop(0, slabs // 2, backward_slabs, 0)
    unfold(slabs - 1, (groups - 1) * BATCH, totals[(groups - 1) % 2])
    staged[...] = jnp.zeros_like(staged)

    def gather(g):
        value = waves[pl.ds(row_ref[g], 1), :]
        pltpu.store(staged.at[pl.ds(source_ref[g], 1), :], value, mask=lane_half == half_ref[g])

    over_live(gather)

    def restore(quad, carry):
        base = pl.multiple_of(quad * 128, 128)
        block = staged[pl.ds(base, 128), :] + pltpu.roll(staged[pl.ds(rows + base, 128), :], 64, 1)
        block = block.T
        for pair in range(2):
            d = quad * 4 + pair * 2
            for c in range(2):
                for t in range(2):
                    line = (pair * 8 + c * 4 + t * 2) * 8
                    first, second = swap_halves(block[line : line + 8], block[line + 8 : line + 16])
                    at = (pl.ds(c * 8, 8), pl.ds(t * 128, 128))
                    out_ref[d, at[0], at[1]] = first
                    out_ref[d + 1, at[0], at[1]] = second
        return carry

    lax.fori_loop(0, devices // 4, restore, 0, unroll=4)


def on_grid(source, row, half, count, sticks, local):
    table = folded_table()
    turned = np.swapaxes(table, 1, 2)
    rows = sticks.shape[0] * 32
    smem = pl.BlockSpec(memory_space=pltpu.SMEM)
    vmem = pl.BlockSpec(memory_space=pltpu.VMEM)
    return pl.pallas_call(
        grid_kernel,
        out_shape=jax.ShapeDtypeStruct(sticks.shape, jnp.float32),
        in_specs=[smem] * 4 + [pl.BlockSpec(memory_space=pl.ANY)] * 4,
        out_specs=vmem,
        scratch_shapes=[
            pltpu.VMEM((COMBOS // 2 * PAD, 128), jnp.float32),
            pltpu.VMEM((COMBOS // 2 * PAD, 128), jnp.float32),
            pltpu.VMEM((2 * RADIX * 128, 128), jnp.float32),
            pltpu.VMEM((2 * RADIX * 128, 128), jnp.float32),
            pltpu.VMEM((2, BATCH * 128, PAD), jnp.bfloat16),
            pltpu.VMEM((2, BATCH * 128, PAD), jnp.bfloat16),
            pltpu.VMEM((BATCH * 128, PAD), jnp.float32),
            pltpu.VMEM((BATCH * 128, PAD), jnp.float32),
            pltpu.VMEM((2 * rows, 128), jnp.float32),
            pltpu.VMEM(local.shape, jnp.float32),
            pltpu.VMEM(table.shape, jnp.bfloat16),
            pltpu.VMEM(table.shape, jnp.bfloat16),
            pltpu.SemaphoreType.DMA((4,)),
        ],
        compiler_params=pltpu.CompilerParams(vmem_limit_bytes=60 * 2**20),
    )(source, row, half, count, sticks, local, jnp.asarray(table), jnp.asarray(turned))


class Layout:
    def __init__(self, tg_size, fft_size, plane_slots):
        self.tg_size, self.fft_size, self.plane_slots = tg_size, fft_size, plane_slots
        self.devices = tg_size * fft_size
        self.chunk = -(-plane_slots // tg_size)
        self.starts = [t * self.chunk // SLOTS * SLOTS for t in range(tg_size)]


def greet(n, fft_size, me):
    barrier = pltpu.get_barrier_semaphore()

    def signal(i, carry):
        other = lax.rem(me + i, n)
        pl.semaphore_signal(
            barrier, inc=1, device_id=(other // fft_size, lax.rem(other, fft_size)), device_id_type=MESH
        )
        return carry

    lax.fori_loop(1, n, signal, 0)
    return lambda: pl.semaphore_wait(barrier, n - 1)


def exchange(n, fft_size, me, source, target, send_sem, recv_sem):
    def copy(i):
        other = lax.rem(me + i, n)
        return pltpu.make_async_remote_copy(
            src_ref=source.at[other], dst_ref=target.at[me], send_sem=send_sem.at[i], recv_sem=recv_sem.at[i],
            device_id=(other // fft_size, lax.rem(other, fft_size)), device_id_type=MESH,
        )

    def start(i, carry):
        copy(i).start()
        return carry

    def wait(i, carry):
        copy(i).wait()
        return carry

    own = pltpu.make_async_copy(source.at[me], target.at[me], send_sem.at[0])

    def begin():
        lax.fori_loop(1, n, start, 0)
        own.start()

    def finish():
        own.wait()
        lax.fori_loop(1, n, wait, 0)

    return begin, finish


def plane_row(layout, owner_ref):
    outside = jnp.full((1, PAD - NZ), 2 * layout.fft_size, jnp.int32)
    owner = jnp.concatenate([owner_ref[...], outside], axis=1).astype(jnp.float32)
    owner = jnp.broadcast_to(owner, (PAD, PAD))
    index = lax.broadcasted_iota(jnp.int32, (PAD, PAD), 0)
    same = (owner == owner.T) & (index < lax.broadcasted_iota(jnp.int32, (PAD, PAD), 1))
    rank = jnp.sum(jnp.where(same, 1.0, 0.0), axis=0, keepdims=True)
    group = jnp.zeros_like(rank)
    offset = jnp.zeros_like(rank)
    for t in range(1, layout.tg_size):
        beyond = rank >= float(t * layout.chunk)
        group = jnp.where(beyond, float(t), group)
        offset = jnp.where(beyond, float(layout.starts[t]), offset)
    return (group * layout.fft_size + owner[:1]) * SLOTS + rank - offset


def plane_pick(row, first):
    index = lax.broadcasted_iota(jnp.int32, (PAD, PAD), 0)
    return jnp.where(index.astype(jnp.float32) + float(first) == row, 1.0, 0.0).astype(jnp.bfloat16)


def plane_tables(pick, table_ref):
    return dot(pick, table_ref[0]).astype(jnp.bfloat16), dot(pick, table_ref[1]).astype(jnp.bfloat16)


def divided(value, divisor):
    quotient = jnp.floor((value + 0.5) * (1.0 / divisor))
    return quotient, value - quotient * divisor


def stick_places(count_ref, column_ref, source_ref, row_ref, half_ref):
    rows = column_ref.shape[0]
    lane = lax.broadcasted_iota(jnp.int32, (8, 128), 1)
    sublane = lax.broadcasted_iota(jnp.int32, (8, 128), 0)
    within = lane % 64
    middle, last = float(ODD // 2), float(FOLD - 1)

    def step(i, carry):
        at = pl.ds(pl.multiple_of(i * 8, 8), 8)
        count = jnp.zeros((8, 128), jnp.int32)
        for r in range(8):
            for h in range(2):
                count = jnp.where((sublane == r) & (lane // 64 == h), count_ref[i * 16 + 2 * r + h], count)
        x, y = divided(column_ref[at, :].astype(jnp.float32), float(NY))
        ax, ay = divided(x, float(RADIX))[1], divided(y, float(RADIX))[1]
        bx, by = divided(x, float(ODD))[1], divided(y, float(ODD))[1]
        negative = (bx > middle) | ((bx == 0.0) & (by > middle))
        bx = jnp.where(negative & (bx > 0.0), ODD - bx, bx)
        by = jnp.where(negative & (by > 0.0), ODD - by, by)
        place = jnp.where(bx == 0.0, by, middle + 1.0 + (bx - 1.0) * ODD + by)
        place = place + jnp.where(negative, float(FOLD), 0.0)
        pair, half = divided(ax * RADIX + ay, 2.0)
        row_ref[at, :] = jnp.where(within < count, pair * PAD + place, last).astype(jnp.int32)
        half = half.astype(jnp.int32)
        half_ref[at, :] = half
        slot_row = i * 8 + sublane
        source = slot_row // 2 * 128 + lane
        source_ref[at, :] = source + jnp.where(slot_row % 2 != half, rows * 64, 0)
        return carry

    lax.fori_loop(0, rows // 8, step, 0)


def lift_kernel(
    layout, coeffs_hbm, owner_ref, count_ref, column_ref, potential_ref, table_hbm, order_hbm,
    out_ref, local_out, source_ref, row_ref, half_ref,
    parts, local_ref, slab, lines, spread, coeffs_ref, table_ref, order_ref, send_sem, recv_sem, slab_sem, load_sem, store_sem,
):
    n, fft_size = layout.devices, layout.fft_size
    tg = lax.axis_index("tg")
    me = tg * fft_size + lax.axis_index("fft")
    loads = [
        pltpu.make_async_copy(source, target, load_sem.at[i])
        for i, (source, target) in enumerate(
            [(coeffs_hbm, coeffs_ref), (table_hbm, table_ref), (order_hbm, order_ref)]
        )
    ]
    for load in loads:
        load.start()
    greeted = greet(n, fft_size, me)

    slabs = []
    for t in range(layout.tg_size):
        start = layout.starts[t]
        count = min(SLOTS, layout.plane_slots - start)
        slabs.append((t, count, pltpu.make_async_copy(
            potential_ref.at[pl.ds(start, count), :], slab.at[pl.ds(0, count), :], slab_sem
        )))
    for t, count, copy in slabs:
        @pl.when(tg == t)
        def _():
            if count < SLOTS:
                slab[...] = jnp.zeros_like(slab)
            copy.start()

    per = PAD // SLOTS
    row = plane_row(layout, owner_ref)
    picks = [plane_pick(row, first * SLOTS) for first in range(0, n, per)]
    loads[1].wait()
    tables = [plane_tables(pick, table_ref) for pick in picks]
    loads[0].wait()
    bands, _, sticks, _ = coeffs_ref.shape
    real = halves(coeffs_ref[:, 0].reshape(bands * sticks, NZ))
    imag = halves(coeffs_ref[:, 1].reshape(bands * sticks, NZ))

    def three(high, low, values):
        return dot_last(high, values[0]) + dot_last(low, values[0]) + dot_last(high, values[1])

    for first in range(0, n, per):
        high, low = tables[first // per]
        cos_high, cos_low = high[:, :NZ], low[:, :NZ]
        sin_high, sin_low = high[:, PAD : PAD + NZ], low[:, PAD : PAD + NZ]
        up_real = three(cos_high, cos_low, real) - three(sin_high, sin_low, imag)
        up_imag = three(sin_high, sin_low, real) + three(cos_high, cos_low, imag)
        parts[first : first + per, :SLOTS] = up_real.reshape(per, SLOTS, bands * sticks)
        parts[first : first + per, SLOTS:] = up_imag.reshape(per, SLOTS, bands * sticks)

    begin, finish = exchange(n, fft_size, me, parts, out_ref, send_sem, recv_sem)
    greeted()
    begin()

    stick_places(count_ref, column_ref, source_ref, row_ref, half_ref)
    loads[2].wait()
    for t, count, copy in slabs:
        @pl.when(tg == t)
        def _():
            copy.wait()

    lines[:, NY:] = jnp.zeros((NX * SLOTS, PAD - NY), jnp.float32)

    def cut(q, carry):
        wide = slab[:, pl.ds(pl.multiple_of(q * 8 * NY, 128), 8 * NY)]
        for r in range(8):
            lines[pl.ds(pl.multiple_of(q * 8 * SLOTS, 8 * SLOTS) + r * SLOTS, SLOTS), :NY] = wide[:, r * NY : (r + 1) * NY]
        return carry

    lax.fori_loop(0, NX // 8, cut, 0)
    order = order_ref[...]

    def reorder(i, carry):
        at = pl.ds(pl.multiple_of(i * 128, 128), 128)
        values = lines[at, :]
        high, low = halves(values)
        rest = (values - high.astype(jnp.float32) - low.astype(jnp.float32)).astype(jnp.bfloat16)
        spread[at, :] = dot(high, order) + dot(low, order) + dot(rest, order)
        return carry

    lax.fori_loop(0, NX * SLOTS // 128, reorder, 0)
    lane_block = lax.broadcasted_iota(jnp.int32, (SLOTS, 128), 1) // RADIX

    def regroup(nx, carry):
        tiles = []
        for mx in range(ODD):
            x = lax.rem(nx * ODD + mx * RADIX, NX)
            at = pl.ds(pl.multiple_of(x * SLOTS, SLOTS), SLOTS)
            tiles.append([spread[at, :128], spread[at, 128:]])
        tiles.append([jnp.zeros((SLOTS, 128), jnp.float32)] * 2)
        tiles = [[tiles[m % 8 + 8 * (h % 2)][m // 8] for h in range(2)] for m in range(16)]
        for bit in (4, 2, 1):
            shift = bit * RADIX
            clear = lane_block % (2 * bit) < bit
            fresh = [[None, None] for _ in range(16)]
            for m in range(16):
                if m & bit:
                    continue
                for h in range(2):
                    a, b = tiles[m][h], tiles[m | bit][h]
                    fresh[m][h] = jnp.where(clear, a, pltpu.roll(b, shift, 1))
                    fresh[m | bit][h] = jnp.where(clear, pltpu.roll(a, 128 - shift, 1), b)
            tiles = fresh
        for ny in range(16):
            local_ref[nx * RADIX + ny, :, :128] = tiles[ny][0]
            local_ref[nx * RADIX + ny, :, 128:] = tiles[ny][1]
        return carry

    lax.fori_loop(0, RADIX, regroup, 0)
    store = pltpu.make_async_copy(local_ref, local_out, store_sem)
    store.start()
    store.wait()
    finish()


def lift(layout, coeffs, owner, count, column, potential):
    bands, _, sticks, _ = coeffs.shape
    index = jax.ShapeDtypeStruct(column.shape, jnp.int32)
    table, order = z_table(), y_order()
    n = layout.devices
    hbm = pl.BlockSpec(memory_space=pl.ANY)
    vmem = pl.BlockSpec(memory_space=pltpu.VMEM)
    return pl.pallas_call(
        functools.partial(lift_kernel, layout),
        out_shape=(
            jax.ShapeDtypeStruct((n, 2 * SLOTS, bands * sticks), jnp.float32),
            jax.ShapeDtypeStruct((COMBOS, SLOTS, PAD), jnp.float32),
            index, index, index,
        ),
        in_specs=[hbm, vmem, pl.BlockSpec(memory_space=pltpu.SMEM), vmem, hbm, hbm, hbm],
        out_specs=(hbm, hbm, vmem, vmem, vmem),
        scratch_shapes=[
            pltpu.VMEM((n, 2 * SLOTS, bands * sticks), jnp.float32),
            pltpu.VMEM((COMBOS, SLOTS, PAD), jnp.float32),
            pltpu.VMEM((SLOTS, NX * NY), jnp.float32),
            pltpu.VMEM((NX * SLOTS, PAD), jnp.float32),
            pltpu.VMEM((NX * SLOTS, PAD), jnp.float32),
            pltpu.VMEM(coeffs.shape, jnp.float32),
            pltpu.VMEM(table.shape, jnp.bfloat16),
            pltpu.VMEM(order.shape, jnp.bfloat16),
            pltpu.SemaphoreType.DMA((n,)),
            pltpu.SemaphoreType.DMA((n,)),
            pltpu.SemaphoreType.DMA,
            pltpu.SemaphoreType.DMA((3,)),
            pltpu.SemaphoreType.DMA,
        ],
        compiler_params=pltpu.CompilerParams(
            collective_id=0, has_side_effects=True, vmem_limit_bytes=60 * 2**20
        ),
    )(coeffs, owner, count, column, potential, jnp.asarray(table), jnp.asarray(order))


def back_kernel(
    layout, worked_ref, owner_ref, count_ref, table_hbm, out_ref, received, table_ref, send_sem, recv_sem, load_sem
):
    n, fft_size = layout.devices, layout.fft_size
    me = lax.axis_index("tg") * fft_size + lax.axis_index("fft")
    begin, finish = exchange(n, fft_size, me, worked_ref, received, send_sem, recv_sem)
    load = pltpu.make_async_copy(table_hbm, table_ref, load_sem)
    load.start()
    greet(n, fft_size, me)()
    begin()
    load.wait()
    per = PAD // SLOTS
    row = plane_row(layout, owner_ref)
    tables = [plane_tables(plane_pick(row, first * SLOTS), table_ref) for first in range(0, n, per)]
    finish()

    bands, _, sticks, _ = out_ref.shape
    out_real = jnp.zeros((bands * sticks, PAD), jnp.float32)
    out_imag = jnp.zeros((bands * sticks, PAD), jnp.float32)

    def three(values, high, low):
        return dot(values[0], high) + dot(values[0], low) + dot(values[1], high)

    for index, first in enumerate(range(0, n, per)):
        high, low = tables[index]
        real = halves(received[first : first + per, :SLOTS].reshape(PAD, bands * sticks).T)
        imag = halves(received[first : first + per, SLOTS:].reshape(PAD, bands * sticks).T)
        cos_high, cos_low = high[:, :PAD], low[:, :PAD]
        sin_high, sin_low = high[:, PAD:], low[:, PAD:]
        out_real += three(real, cos_high, cos_low) + three(imag, sin_high, sin_low)
        out_imag += three(imag, cos_high, cos_low) - three(real, sin_high, sin_low)
    live = lax.broadcasted_iota(jnp.int32, (bands, sticks, NZ), 1) < count_ref[me]
    out_ref[:, 0] = jnp.where(live, out_real[:, :NZ].reshape(bands, sticks, NZ), 0.0)
    out_ref[:, 1] = jnp.where(live, out_imag[:, :NZ].reshape(bands, sticks, NZ), 0.0)


def lower(layout, worked, owner, count, shape):
    n = layout.devices
    table = z_table()
    hbm = pl.BlockSpec(memory_space=pltpu.HBM)
    vmem = pl.BlockSpec(memory_space=pltpu.VMEM)
    return pl.pallas_call(
        functools.partial(back_kernel, layout),
        out_shape=jax.ShapeDtypeStruct(shape, jnp.float32),
        in_specs=[hbm, vmem, pl.BlockSpec(memory_space=pltpu.SMEM), hbm],
        out_specs=vmem,
        scratch_shapes=[
            pltpu.VMEM(worked.shape, jnp.float32),
            pltpu.VMEM(table.shape, jnp.bfloat16),
            pltpu.SemaphoreType.DMA((n,)),
            pltpu.SemaphoreType.DMA((n,)),
            pltpu.SemaphoreType.DMA,
        ],
        compiler_params=pltpu.CompilerParams(
            collective_id=1, has_side_effects=True, vmem_limit_bytes=40 * 2**20
        ),
    )(worked, owner, count, jnp.asarray(table))


def per_device(coeffs, stick_count, stick_column, plane_owner, potential):
    layout = Layout(lax.axis_size("tg"), lax.axis_size("fft"), potential.shape[0])
    turned = jnp.swapaxes(coeffs, 2, 3)
    owner = plane_owner.reshape(1, NZ)
    column = stick_column.reshape(-1, 128)
    sticks, local, *places = lift(layout, turned, owner, stick_count, column, potential)
    places = [place.reshape(-1) for place in places]
    worked = on_grid(*places, stick_count, sticks, local)
    applied = lower(layout, worked, owner, stick_count, turned.shape)
    return jnp.swapaxes(applied, 2, 3)


def solution(mesh):
    in_specs = (P(None, None, None, ("tg", "fft")), P(), P(), P(), P("fft", None))
    out_specs = P(None, None, None, ("tg", "fft"))
    return jax.shard_map(
        per_device, mesh=mesh, in_specs=in_specs, out_specs=out_specs, check_vma=False
    )
```

```python
import functools
import math

import jax
import jax.numpy as jnp
import ml_dtypes
import numpy as np
from jax import lax
from jax.experimental import pallas as pl
from jax.experimental.pallas import tpu as pltpu
from jax.sharding import PartitionSpec as P

NX = 240
NY = 240
NZ = 240
PAD = 256
FOLD = 128
LANES = 64
RADIX = 16
ODD = 15
COMBOS = RADIX * RADIX
SLOTS = 8
GROUP = 8
UNROLL_Y = 2
BATCH = 4
MESH = pl.DeviceIdType.MESH


def split_table(table):
    table = table.astype(np.float32)
    high = table.astype(ml_dtypes.bfloat16)
    low = (table - high.astype(np.float32)).astype(ml_dtypes.bfloat16)
    return np.stack([high, low])


def z_table():
    indices = np.arange(NZ)
    angles = (indices[:, None] * indices[None, :] % NZ) * (2.0 * math.pi / NZ)
    table = np.zeros((PAD, 2 * PAD))
    table[:NZ, :NZ] = np.cos(angles) / math.sqrt(NZ)
    table[:NZ, PAD : PAD + NZ] = np.sin(angles) / math.sqrt(NZ)
    return split_table(table)


def folded_table():
    first = np.arange(ODD)
    table = np.zeros((PAD, PAD))
    for bx in range(ODD // 2 + 1):
        for by in range(ODD if bx else ODD // 2 + 1):
            i = ODD // 2 + 1 + (bx - 1) * ODD + by if bx else by
            angles = ((bx * first[:, None] + by * first[None, :]) % ODD) * (2.0 * math.pi / ODD)
            wide = np.zeros((2, RADIX, RADIX))
            wide[0, :ODD, :ODD] = np.cos(angles)
            wide[1, :ODD, :ODD] = -np.sin(angles)
            table[i] = wide[0].reshape(-1) / NX
            table[FOLD + i] = wide[1].reshape(-1) / NX
    return split_table(table)


def y_order():
    order = np.zeros((PAD, PAD), np.float32)
    y = np.arange(NY)
    order[y, (-y) % RADIX * RADIX + y % ODD] = 1.0
    return order.astype(ml_dtypes.bfloat16)


def halves(values):
    high = values.astype(jnp.bfloat16)
    low = (values - high.astype(jnp.float32)).astype(jnp.bfloat16)
    return high, low


def dot(a, b):
    return jnp.dot(a, b, preferred_element_type=jnp.float32)


def dot_last(a, b):
    return lax.dot_general(a, b, (((1,), (1,)), ((), ())), preferred_element_type=jnp.float32)


def butterfly(real, imag, sign):
    def four(xs):
        (ar, ai), (br, bi), (cr, ci), (dr, di) = xs
        er, ei, fr, fi = ar + cr, ai + ci, ar - cr, ai - ci
        gr, gi, hr, hi = br + dr, bi + di, br - dr, bi - di
        if sign > 0:
            return [(er + gr, ei + gi), (fr - hi, fi + hr), (er - gr, ei - gi), (fr + hi, fi - hr)]
        return [(er + gr, ei + gi), (fr + hi, fi - hr), (er - gr, ei - gi), (fr - hi, fi + hr)]

    def turn(x, power):
        r, i = x
        root = math.sqrt(0.5)
        if power == 0:
            return x
        if power == 4:
            return (-i, r) if sign > 0 else (i, -r)
        if power == 2:
            return ((r - i) * root, (r + i) * root) if sign > 0 else ((r + i) * root, (i - r) * root)
        if power == 6:
            return ((r + i) * -root, (r - i) * root) if sign > 0 else ((i - r) * root, (r + i) * -root)
        c = math.cos(2 * math.pi * power / 16)
        s = math.sin(2 * math.pi * power / 16) * sign
        return r * c - i * s, r * s + i * c

    inner = [four([(real[4 * n1 + n2], imag[4 * n1 + n2]) for n1 in range(4)]) for n2 in range(4)]
    out_real, out_imag = [None] * 16, [None] * 16
    for k1 in range(4):
        outer = four([turn(inner[n2][k1], n2 * k1) for n2 in range(4)])
        for k2 in range(4):
            out_real[k1 + 4 * k2], out_imag[k1 + 4 * k2] = outer[k2]
    return out_real, out_imag


def swap_halves(first, second):
    lower = lax.broadcasted_iota(jnp.int32, first.shape, first.ndim - 1) < 64
    first_turned = pltpu.roll(first, 64, first.ndim - 1)
    second_turned = pltpu.roll(second, 64, second.ndim - 1)
    return jnp.where(lower, first, second_turned), jnp.where(lower, first_turned, second)


def grid_kernel(
    source_ref, row_ref, half_ref, count_ref, sticks_hbm, local_hbm, table_hbm, turned_hbm, out_ref,
    columns, waves, ring, spare, prep_even, prep_odd, total_even, total_odd, staged, local_ref, table_ref, turned_ref, load_sem,
):
    loads = [
        pltpu.make_async_copy(source, target, load_sem.at[i])
        for i, (source, target) in enumerate(
            [(sticks_hbm, out_ref), (table_hbm, table_ref), (local_hbm, local_ref), (turned_hbm, turned_ref)]
        )
    ]
    for load in loads:
        load.start()
    devices = out_ref.shape[0]
    rows = devices * 32
    lane_half = lax.broadcasted_iota(jnp.int32, (1, 128), 1) // 64

    def clear(i, carry):
        columns[pl.ds(pl.multiple_of(i * PAD, PAD), PAD), :] = jnp.zeros((PAD, 128), jnp.float32)
        return carry

    lax.fori_loop(0, COMBOS // 2, clear, 0)
    loads[0].wait()

    def arrange(quad, carry):
        lines = [None] * 16
        for pair in range(2):
            d = quad * 4 + pair * 2
            for c in range(2):
                for t in range(2):
                    at = (pl.ds(c * 8, 8), pl.ds(t * 128, 128))
                    even, odd = swap_halves(out_ref[d, at[0], at[1]], out_ref[d + 1, at[0], at[1]])
                    lines[pair * 8 + c * 4 + t * 2] = even
                    lines[pair * 8 + c * 4 + t * 2 + 1] = odd
        block = jnp.concatenate(lines, axis=0).T
        base = pl.multiple_of(quad * 128, 128)
        staged[pl.ds(base, 128), :] = block
        staged[pl.ds(rows + base, 128), :] = pltpu.roll(block, 64, 1)
        return carry

    lax.fori_loop(0, devices // 4, arrange, 0, unroll=4)

    def over_live(work):
        def per_device(d, carry):
            def per_group(i, inner):
                for j in range(GROUP):
                    work(d * 64 + i * GROUP + j)
                return inner

            return lax.fori_loop(0, (count_ref[d] + GROUP - 1) // GROUP, per_group, carry)

        lax.fori_loop(0, devices, per_device, 0)

    def scatter(g):
        value = staged[pl.ds(source_ref[g], 1), :]
        pltpu.store(columns.at[pl.ds(row_ref[g], 1), :], value, mask=lane_half == half_ref[g])

    over_live(scatter)

    def folded(i, ax):
        base = pl.multiple_of((ax * (RADIX // 2) + i) * PAD, PAD)
        low_half = columns[pl.ds(base, FOLD), :].T
        high_half = columns[pl.ds(base + FOLD, FOLD), :].T
        odd = []
        for h in range(2):
            re, im = slice(h * 64, h * 64 + 32), slice(h * 64 + 32, h * 64 + 64)
            odd += [low_half[im] - high_half[im], high_half[re] - low_half[re]]
        return jnp.concatenate([low_half + high_half, jnp.concatenate(odd, axis=0)], axis=1)

    def three(high, low, table):
        return dot(high, table[0]) + dot(high, table[1]) + dot(low, table[0])

    def prepare(i, first, prep):
        for k in range(BATCH):
            high, low = halves(folded(i, first + k))
            prep[0, k * 128 : (k + 1) * 128, :] = high
            prep[1, k * 128 : (k + 1) * 128, :] = low

    def forward(ring, first, prep):
        total = three(prep[0], prep[1], table_ref)
        for l in range(2):
            at = pl.ds((l * RADIX + first) * 128, BATCH * 128)
            ring[at, :] = total[:, l * 128 : (l + 1) * 128]

    def in_ring(unit, k, c):
        h, b, l = unit // 8, unit // 2 % 4, unit % 2
        return pl.ds((l * RADIX + k) * 128 + h * 64 + c * 32 + b * 8, 8)

    def in_grid(i, unit, k, c):
        h, b, l = unit // 8, unit // 2 % 4, unit % 2
        base = pl.multiple_of(2 * i * LANES, 128)
        return pl.ds(base + (l * COMBOS + k * RADIX + h) * LANES + c * 32 + b * 8, 8)

    def forward_x(ring, i, unit):
        real = [ring[in_ring(unit, k, 0), :] for k in range(RADIX)]
        imag = [ring[in_ring(unit, k, 1), :] for k in range(RADIX)]
        real, imag = butterfly(real, imag, 1)
        for k in range(RADIX):
            waves[in_grid(i, unit, k, 0), :] = real[k]
            waves[in_grid(i, unit, k, 1), :] = imag[k]

    def backward_x(ring, i, unit):
        real = [columns[in_grid(i, unit, k, 0), :] for k in range(RADIX)]
        imag = [columns[in_grid(i, unit, k, 1), :] for k in range(RADIX)]
        real, imag = butterfly(real, imag, -1)
        for k in range(RADIX):
            ring[in_ring(unit, k, 0), :] = real[k]
            ring[in_ring(unit, k, 1), :] = imag[k]

    def backward(ring, start, total):
        values = jnp.concatenate(
            [ring[pl.ds((l * RADIX + start) * 128, BATCH * 128), :] for l in range(2)], axis=1
        )
        total[...] = three(*halves(values), turned_ref)

    def unfold(i, start, total):
        for k in range(BATCH):
            cosine, sine = total[k * 128 : (k + 1) * 128, :FOLD], total[k * 128 : (k + 1) * 128, FOLD:]
            first, second = [], []
            for h in range(2):
                re, im = slice(h * 64, h * 64 + 32), slice(h * 64 + 32, h * 64 + 64)
                first += [cosine[re] - sine[im], cosine[im] + sine[re]]
                second += [cosine[re] + sine[im], cosine[im] - sine[re]]
            base = pl.multiple_of(((start + k) * (RADIX // 2) + i) * PAD, PAD)
            waves[pl.ds(base, FOLD), :] = jnp.concatenate(first, axis=0).T
            waves[pl.ds(base + FOLD, FOLD), :] = jnp.concatenate(second, axis=0).T

    slabs = RADIX // 2

    preps, totals = (prep_even, prep_odd), (total_even, total_odd)
    groups = RADIX // BATCH

    def forward_group(i, q, target):
        prepare(jnp.minimum(i + (q + 1) // groups, slabs - 1), (q + 1) % groups * BATCH, preps[(q + 1) % 2])
        forward(target, q * BATCH, preps[q % 2])

    def forward_step(i, here, there):
        for j in range(RADIX):
            if j % BATCH == 0:
                forward_group(i + 1, j // BATCH, there)
            forward_x(here, i, j)

    def forward_slabs(t, carry):
        forward_step(2 * t, ring, spare)
        forward_step(2 * t + 1, spare, ring)
        return carry

    loads[1].wait()
    prepare(0, 0, prep_even)
    for q in range(groups):
        forward_group(0, q, ring)
    lax.fori_loop(0, slabs // 2 - 1, forward_slabs, 0)
    forward_step(slabs - 2, ring, spare)
    for j in range(RADIX):
        forward_x(spare, slabs - 1, j)

    def along_y(ax, carry):
        for l in range(2):
            lanes = pl.ds(l * 128, 128)
            for b in range(4):
                def at(k, c):
                    base = pl.multiple_of((l * COMBOS + ax * RADIX) * LANES, LANES)
                    return pl.ds(base + k * LANES + c * 32 + b * 8, 8)

                real = [waves[at(k, 0), :] for k in range(RADIX)]
                imag = [waves[at(k, 1), :] for k in range(RADIX)]
                real, imag = butterfly(real, imag, 1)
                local = [local_ref[ax * RADIX + k, :, lanes] for k in range(RADIX)]
                real = [value * local[k] for k, value in enumerate(real)]
                imag = [value * local[k] for k, value in enumerate(imag)]
                real, imag = butterfly(real, imag, -1)
                for k in range(RADIX):
                    columns[at(k, 0), :] = real[k]
                    columns[at(k, 1), :] = imag[k]
        return carry

    loads[2].wait()
    loads[3].wait()
    lax.fori_loop(0, RADIX, along_y, 0, unroll=UNROLL_Y)

    for j in range(RADIX):
        backward_x(ring, 0, j)

    def backward_step(i, here, there):
        for j in range(RADIX):
            if j % BATCH == 0:
                q = j // BATCH
                unfold(i if q else jnp.maximum(i - 1, 0), (q - 1) % groups * BATCH, totals[(q - 1) % 2])
                backward(here, j, totals[q % 2])
            backward_x(there, jnp.minimum(i + 1, slabs - 1), j)

    def backward_slabs(t, carry):
        backward_step(2 * t, ring, spare)
        backward_step(2 * t + 1, spare, ring)
        return carry

    lax.fori_loop(0, slabs // 2, backward_slabs, 0)
    unfold(slabs - 1, (groups - 1) * BATCH, totals[(groups - 1) % 2])
    staged[...] = jnp.zeros_like(staged)

    def gather(g):
        value = waves[pl.ds(row_ref[g], 1), :]
        pltpu.store(staged.at[pl.ds(source_ref[g], 1), :], value, mask=lane_half == half_ref[g])

    over_live(gather)

    def restore(quad, carry):
        base = pl.multiple_of(quad * 128, 128)
        block = staged[pl.ds(base, 128), :] + pltpu.roll(staged[pl.ds(rows + base, 128), :], 64, 1)
        block = block.T
        for pair in range(2):
            d = quad * 4 + pair * 2
            for c in range(2):
                for t in range(2):
                    line = (pair * 8 + c * 4 + t * 2) * 8
                    first, second = swap_halves(block[line : line + 8], block[line + 8 : line + 16])
                    at = (pl.ds(c * 8, 8), pl.ds(t * 128, 128))
                    out_ref[d, at[0], at[1]] = first
                    out_ref[d + 1, at[0], at[1]] = second
        return carry

    lax.fori_loop(0, devices // 4, restore, 0, unroll=4)


def on_grid(source, row, half, count, sticks, local):
    table = folded_table()
    turned = np.swapaxes(table, 1, 2)
    rows = sticks.shape[0] * 32
    smem = pl.BlockSpec(memory_space=pltpu.SMEM)
    vmem = pl.BlockSpec(memory_space=pltpu.VMEM)
    return pl.pallas_call(
        grid_kernel,
        out_shape=jax.ShapeDtypeStruct(sticks.shape, jnp.float32),
        in_specs=[smem] * 4 + [pl.BlockSpec(memory_space=pl.ANY)] * 4,
        out_specs=vmem,
        scratch_shapes=[
            pltpu.VMEM((COMBOS // 2 * PAD, 128), jnp.float32),
            pltpu.VMEM((COMBOS // 2 * PAD, 128), jnp.float32),
            pltpu.VMEM((2 * RADIX * 128, 128), jnp.float32),
            pltpu.VMEM((2 * RADIX * 128, 128), jnp.float32),
            pltpu.VMEM((2, BATCH * 128, PAD), jnp.bfloat16),
            pltpu.VMEM((2, BATCH * 128, PAD), jnp.bfloat16),
            pltpu.VMEM((BATCH * 128, PAD), jnp.float32),
            pltpu.VMEM((BATCH * 128, PAD), jnp.float32),
            pltpu.VMEM((2 * rows, 128), jnp.float32),
            pltpu.VMEM(local.shape, jnp.float32),
            pltpu.VMEM(table.shape, jnp.bfloat16),
            pltpu.VMEM(table.shape, jnp.bfloat16),
            pltpu.SemaphoreType.DMA((4,)),
        ],
        compiler_params=pltpu.CompilerParams(vmem_limit_bytes=60 * 2**20),
    )(source, row, half, count, sticks, local, jnp.asarray(table), jnp.asarray(turned))


class Layout:
    def __init__(self, tg_size, fft_size, plane_slots):
        self.tg_size, self.fft_size, self.plane_slots = tg_size, fft_size, plane_slots
        self.devices = tg_size * fft_size
        self.chunk = -(-plane_slots // tg_size)
        self.starts = [t * self.chunk // SLOTS * SLOTS for t in range(tg_size)]


def greet(n, fft_size, me):
    barrier = pltpu.get_barrier_semaphore()

    def signal(i, carry):
        other = lax.rem(me + i, n)
        pl.semaphore_signal(
            barrier, inc=1, device_id=(other // fft_size, lax.rem(other, fft_size)), device_id_type=MESH
        )
        return carry

    lax.fori_loop(1, n, signal, 0)
    return lambda: pl.semaphore_wait(barrier, n - 1)


def exchange(n, fft_size, me, source, target, send_sem, recv_sem):
    def copy(i):
        other = lax.rem(me + i, n)
        return pltpu.make_async_remote_copy(
            src_ref=source.at[other], dst_ref=target.at[me], send_sem=send_sem.at[i], recv_sem=recv_sem.at[i],
            device_id=(other // fft_size, lax.rem(other, fft_size)), device_id_type=MESH,
        )

    def start(i, carry):
        copy(i).start()
        return carry

    def wait(i, carry):
        copy(i).wait()
        return carry

    own = pltpu.make_async_copy(source.at[me], target.at[me], send_sem.at[0])

    def begin():
        lax.fori_loop(1, n, start, 0)
        own.start()

    def finish():
        own.wait()
        lax.fori_loop(1, n, wait, 0)

    return begin, finish


def plane_row(layout, owner_ref):
    outside = jnp.full((1, PAD - NZ), 2 * layout.fft_size, jnp.int32)
    owner = jnp.concatenate([owner_ref[...], outside], axis=1).astype(jnp.float32)
    owner = jnp.broadcast_to(owner, (PAD, PAD))
    index = lax.broadcasted_iota(jnp.int32, (PAD, PAD), 0)
    same = (owner == owner.T) & (index < lax.broadcasted_iota(jnp.int32, (PAD, PAD), 1))
    rank = jnp.sum(jnp.where(same, 1.0, 0.0), axis=0, keepdims=True)
    group = jnp.zeros_like(rank)
    offset = jnp.zeros_like(rank)
    for t in range(1, layout.tg_size):
        beyond = rank >= float(t * layout.chunk)
        group = jnp.where(beyond, float(t), group)
        offset = jnp.where(beyond, float(layout.starts[t]), offset)
    return (group * layout.fft_size + owner[:1]) * SLOTS + rank - offset


def plane_pick(row, first):
    index = lax.broadcasted_iota(jnp.int32, (PAD, PAD), 0)
    return jnp.where(index.astype(jnp.float32) + float(first) == row, 1.0, 0.0).astype(jnp.bfloat16)


def plane_tables(pick, table_ref):
    return dot(pick, table_ref[0]).astype(jnp.bfloat16), dot(pick, table_ref[1]).astype(jnp.bfloat16)


def divided(value, divisor):
    quotient = jnp.floor((value + 0.5) * (1.0 / divisor))
    return quotient, value - quotient * divisor


def stick_places(count_ref, column_ref, source_ref, row_ref, half_ref):
    rows = column_ref.shape[0]
    lane = lax.broadcasted_iota(jnp.int32, (8, 128), 1)
    sublane = lax.broadcasted_iota(jnp.int32, (8, 128), 0)
    within = lane % 64
    middle, last = float(ODD // 2), float(FOLD - 1)

    def step(i, carry):
        at = pl.ds(pl.multiple_of(i * 8, 8), 8)
        count = jnp.zeros((8, 128), jnp.int32)
        for r in range(8):
            for h in range(2):
                count = jnp.where((sublane == r) & (lane // 64 == h), count_ref[i * 16 + 2 * r + h], count)
        x, y = divided(column_ref[at, :].astype(jnp.float32), float(NY))
        ax, ay = divided(x, float(RADIX))[1], divided(y, float(RADIX))[1]
        bx, by = divided(x, float(ODD))[1], divided(y, float(ODD))[1]
        negative = (bx > middle) | ((bx == 0.0) & (by > middle))
        bx = jnp.where(negative & (bx > 0.0), ODD - bx, bx)
        by = jnp.where(negative & (by > 0.0), ODD - by, by)
        place = jnp.where(bx == 0.0, by, middle + 1.0 + (bx - 1.0) * ODD + by)
        place = place + jnp.where(negative, float(FOLD), 0.0)
        pair, half = divided(ax * RADIX + ay, 2.0)
        row_ref[at, :] = jnp.where(within < count, pair * PAD + place, last).astype(jnp.int32)
        half = half.astype(jnp.int32)
        half_ref[at, :] = half
        slot_row = i * 8 + sublane
        source = slot_row // 2 * 128 + lane
        source_ref[at, :] = source + jnp.where(slot_row % 2 != half, rows * 64, 0)
        return carry

    lax.fori_loop(0, rows // 8, step, 0)


def lift_kernel(
    layout, coeffs_hbm, owner_ref, count_ref, column_ref, potential_ref, table_hbm, order_hbm,
    out_ref, local_out, source_ref, row_ref, half_ref,
    parts, local_ref, slab, lines, spread, coeffs_ref, table_ref, order_ref, send_sem, recv_sem, slab_sem, load_sem, store_sem,
):
    n, fft_size = layout.devices, layout.fft_size
    tg = lax.axis_index("tg")
    me = tg * fft_size + lax.axis_index("fft")
    loads = [
        pltpu.make_async_copy(source, target, load_sem.at[i])
        for i, (source, target) in enumerate(
            [(coeffs_hbm, coeffs_ref), (table_hbm, table_ref), (order_hbm, order_ref)]
        )
    ]
    for load in loads:
        load.start()
    greeted = greet(n, fft_size, me)

    slabs = []
    for t in range(layout.tg_size):
        start = layout.starts[t]
        count = min(SLOTS, layout.plane_slots - start)
        slabs.append((t, count, pltpu.make_async_copy(
            potential_ref.at[pl.ds(start, count), :], slab.at[pl.ds(0, count), :], slab_sem
        )))
    for t, count, copy in slabs:
        @pl.when(tg == t)
        def _():
            if count < SLOTS:
                slab[...] = jnp.zeros_like(slab)
            copy.start()

    per = PAD // SLOTS
    row = plane_row(layout, owner_ref)
    picks = [plane_pick(row, first * SLOTS) for first in range(0, n, per)]
    loads[1].wait()
    tables = [plane_tables(pick, table_ref) for pick in picks]
    loads[0].wait()
    bands, _, sticks, _ = coeffs_ref.shape
    real = halves(coeffs_ref[:, 0].reshape(bands * sticks, NZ))
    imag = halves(coeffs_ref[:, 1].reshape(bands * sticks, NZ))

    def three(high, low, values):
        return dot_last(high, values[0]) + dot_last(low, values[0]) + dot_last(high, values[1])

    for first in range(0, n, per):
        high, low = tables[first // per]
        cos_high, cos_low = high[:, :NZ], low[:, :NZ]
        sin_high, sin_low = high[:, PAD : PAD + NZ], low[:, PAD : PAD + NZ]
        up_real = three(cos_high, cos_low, real) - three(sin_high, sin_low, imag)
        up_imag = three(sin_high, sin_low, real) + three(cos_high, cos_low, imag)
        parts[first : first + per, :SLOTS] = up_real.reshape(per, SLOTS, bands * sticks)
        parts[first : first + per, SLOTS:] = up_imag.reshape(per, SLOTS, bands * sticks)

    begin, finish = exchange(n, fft_size, me, parts, out_ref, send_sem, recv_sem)
    greeted()
    begin()

    stick_places(count_ref, column_ref, source_ref, row_ref, half_ref)
    loads[2].wait()
    for t, count, copy in slabs:
        @pl.when(tg == t)
        def _():
            copy.wait()

    lines[:, NY:] = jnp.zeros((NX * SLOTS, PAD - NY), jnp.float32)

    def cut(q, carry):
        wide = slab[:, pl.ds(pl.multiple_of(q * 8 * NY, 128), 8 * NY)]
        for r in range(8):
            lines[pl.ds(pl.multiple_of(q * 8 * SLOTS, 8 * SLOTS) + r * SLOTS, SLOTS), :NY] = wide[:, r * NY : (r + 1) * NY]
        return carry

    lax.fori_loop(0, NX // 8, cut, 0)
    order = order_ref[...]

    def reorder(i, carry):
        at = pl.ds(pl.multiple_of(i * 128, 128), 128)
        values = lines[at, :]
        high, low = halves(values)
        rest = (values - high.astype(jnp.float32) - low.astype(jnp.float32)).astype(jnp.bfloat16)
        spread[at, :] = dot(high, order) + dot(low, order) + dot(rest, order)
        return carry

    lax.fori_loop(0, NX * SLOTS // 128, reorder, 0)
    lane_block = lax.broadcasted_iota(jnp.int32, (SLOTS, 128), 1) // RADIX

    def regroup(nx, carry):
        tiles = []
        for mx in range(ODD):
            x = lax.rem(nx * ODD + mx * RADIX, NX)
            at = pl.ds(pl.multiple_of(x * SLOTS, SLOTS), SLOTS)
            tiles.append([spread[at, :128], spread[at, 128:]])
        tiles.append([jnp.zeros((SLOTS, 128), jnp.float32)] * 2)
        tiles = [[tiles[m % 8 + 8 * (h % 2)][m // 8] for h in range(2)] for m in range(16)]
        for bit in (4, 2, 1):
            shift = bit * RADIX
            clear = lane_block % (2 * bit) < bit
            fresh = [[None, None] for _ in range(16)]
            for m in range(16):
                if m & bit:
                    continue
                for h in range(2):
                    a, b = tiles[m][h], tiles[m | bit][h]
                    fresh[m][h] = jnp.where(clear, a, pltpu.roll(b, shift, 1))
                    fresh[m | bit][h] = jnp.where(clear, pltpu.roll(a, 128 - shift, 1), b)
            tiles = fresh
        for ny in range(16):
            local_ref[nx * RADIX + ny, :, :128] = tiles[ny][0]
            local_ref[nx * RADIX + ny, :, 128:] = tiles[ny][1]
        return carry

    lax.fori_loop(0, RADIX, regroup, 0)
    store = pltpu.make_async_copy(local_ref, local_out, store_sem)
    store.start()
    store.wait()
    finish()


def lift(layout, coeffs, owner, count, column, potential):
    bands, _, sticks, _ = coeffs.shape
    index = jax.ShapeDtypeStruct(column.shape, jnp.int32)
    table, order = z_table(), y_order()
    n = layout.devices
    hbm = pl.BlockSpec(memory_space=pl.ANY)
    vmem = pl.BlockSpec(memory_space=pltpu.VMEM)
    return pl.pallas_call(
        functools.partial(lift_kernel, layout),
        out_shape=(
            jax.ShapeDtypeStruct((n, 2 * SLOTS, bands * sticks), jnp.float32),
            jax.ShapeDtypeStruct((COMBOS, SLOTS, PAD), jnp.float32),
            index, index, index,
        ),
        in_specs=[hbm, vmem, pl.BlockSpec(memory_space=pltpu.SMEM), vmem, hbm, hbm, hbm],
        out_specs=(hbm, hbm, vmem, vmem, vmem),
        scratch_shapes=[
            pltpu.VMEM((n, 2 * SLOTS, bands * sticks), jnp.float32),
            pltpu.VMEM((COMBOS, SLOTS, PAD), jnp.float32),
            pltpu.VMEM((SLOTS, NX * NY), jnp.float32),
            pltpu.VMEM((NX * SLOTS, PAD), jnp.float32),
            pltpu.VMEM((NX * SLOTS, PAD), jnp.float32),
            pltpu.VMEM(coeffs.shape, jnp.float32),
            pltpu.VMEM(table.shape, jnp.bfloat16),
            pltpu.VMEM(order.shape, jnp.bfloat16),
            pltpu.SemaphoreType.DMA((n,)),
            pltpu.SemaphoreType.DMA((n,)),
            pltpu.SemaphoreType.DMA,
            pltpu.SemaphoreType.DMA((3,)),
            pltpu.SemaphoreType.DMA,
        ],
        compiler_params=pltpu.CompilerParams(
            collective_id=0, has_side_effects=True, vmem_limit_bytes=60 * 2**20
        ),
    )(coeffs, owner, count, column, potential, jnp.asarray(table), jnp.asarray(order))


def back_kernel(
    layout, worked_ref, owner_ref, count_ref, table_hbm, out_ref, received, table_ref, send_sem, recv_sem, load_sem
):
    n, fft_size = layout.devices, layout.fft_size
    me = lax.axis_index("tg") * fft_size + lax.axis_index("fft")
    begin, finish = exchange(n, fft_size, me, worked_ref, received, send_sem, recv_sem)
    load = pltpu.make_async_copy(table_hbm, table_ref, load_sem)
    load.start()
    greet(n, fft_size, me)()
    begin()
    load.wait()
    per = PAD // SLOTS
    row = plane_row(layout, owner_ref)
    tables = [plane_tables(plane_pick(row, first * SLOTS), table_ref) for first in range(0, n, per)]
    finish()

    bands, _, sticks, _ = out_ref.shape
    out_real = jnp.zeros((bands * sticks, PAD), jnp.float32)
    out_imag = jnp.zeros((bands * sticks, PAD), jnp.float32)

    def three(values, high, low):
        return dot(values[0], high) + dot(values[0], low) + dot(values[1], high)

    for index, first in enumerate(range(0, n, per)):
        high, low = tables[index]
        real = halves(received[first : first + per, :SLOTS].reshape(PAD, bands * sticks).T)
        imag = halves(received[first : first + per, SLOTS:].reshape(PAD, bands * sticks).T)
        cos_high, cos_low = high[:, :PAD], low[:, :PAD]
        sin_high, sin_low = high[:, PAD:], low[:, PAD:]
        out_real += three(real, cos_high, cos_low) + three(imag, sin_high, sin_low)
        out_imag += three(imag, cos_high, cos_low) - three(real, sin_high, sin_low)
    live = lax.broadcasted_iota(jnp.int32, (bands, sticks, NZ), 1) < count_ref[me]
    out_ref[:, 0] = jnp.where(live, out_real[:, :NZ].reshape(bands, sticks, NZ), 0.0)
    out_ref[:, 1] = jnp.where(live, out_imag[:, :NZ].reshape(bands, sticks, NZ), 0.0)


def lower(layout, worked, owner, count, shape):
    n = layout.devices
    table = z_table()
    hbm = pl.BlockSpec(memory_space=pltpu.HBM)
    vmem = pl.BlockSpec(memory_space=pltpu.VMEM)
    return pl.pallas_call(
        functools.partial(back_kernel, layout),
        out_shape=jax.ShapeDtypeStruct(shape, jnp.float32),
        in_specs=[hbm, vmem, pl.BlockSpec(memory_space=pltpu.SMEM), hbm],
        out_specs=vmem,
        scratch_shapes=[
            pltpu.VMEM(worked.shape, jnp.float32),
            pltpu.VMEM(table.shape, jnp.bfloat16),
            pltpu.SemaphoreType.DMA((n,)),
            pltpu.SemaphoreType.DMA((n,)),
            pltpu.SemaphoreType.DMA,
        ],
        compiler_params=pltpu.CompilerParams(
            collective_id=1, has_side_effects=True, vmem_limit_bytes=53 * 2**20
        ),
    )(worked, owner, count, jnp.asarray(table))


def per_device(coeffs, stick_count, stick_column, plane_owner, potential):
    layout = Layout(lax.axis_size("tg"), lax.axis_size("fft"), potential.shape[0])
    turned = jnp.swapaxes(coeffs, 2, 3)
    owner = plane_owner.reshape(1, NZ)
    column = stick_column.reshape(-1, 128)
    sticks, local, *places = lift(layout, turned, owner, stick_count, column, potential)
    places = [place.reshape(-1) for place in places]
    worked = on_grid(*places, stick_count, sticks, local)
    applied = lower(layout, worked, owner, stick_count, turned.shape)
    return jnp.swapaxes(applied, 2, 3)


def solution(mesh):
    in_specs = (P(None, None, None, ("tg", "fft")), P(), P(), P(), P("fft", None))
    out_specs = P(None, None, None, ("tg", "fft"))
    return jax.shard_map(
        per_device, mesh=mesh, in_specs=in_specs, out_specs=out_specs, check_vma=False
    )
```
